32 devices in a mesh: fsdp: 32 (over z, y, x, core).
Axes of the slice: x: 2, y: 2, z: 4, core: 2. Of those that a mesh axis runs over, the one named last changes fastest.
Arguments:
- tokens: bfloat16 [4096, 768], P('fsdp'), may hold values from -6 to 6
- seq_lengths: int32 [32, 8], P('fsdp'), may hold values from 1 to 64, 128 in all within a row
- cotangent: bfloat16 [4096, 768], P('fsdp'), may hold values from -6 to 6
- wide_weights: float32 [768, 6144], P('fsdp'), may hold values from -2 to 2
- proj_weights: float32 [3072, 768], P('fsdp'), may hold values from -0.109375 to 0.109375
- vector_params: float32 [12, 768], P(None, 'fsdp'), may hold values from -1 to 1.5
- wide_moments: float32 [2, 768, 6144], P(None, 'fsdp'), may hold values from -0.16 to 0.16, as said below
- proj_moments: float32 [2, 3072, 768], P(None, 'fsdp'), may hold values from -0.16 to 0.16, as said below
- vector_moments: float32 [2, 12, 768], P(None, None, 'fsdp'), may hold values from -0.16 to 0.16, as said below
Outputs:
- block_output: bfloat16 [4096, 768], P('fsdp')
- tokens_grad: bfloat16 [4096, 768], P('fsdp')
- wide_grad: float32 [768, 6144], P('fsdp')
- proj_grad: float32 [3072, 768], P('fsdp')
- vector_grad: float32 [12, 768], P(None, 'fsdp')
- wide_new: float32 [768, 6144], P('fsdp')
- proj_new: float32 [3072, 768], P('fsdp')
- vector_new: float32 [12, 768], P(None, 'fsdp')
- wide_moments_new: float32 [2, 768, 6144], P(None, 'fsdp')
- proj_moments_new: float32 [2, 3072, 768], P(None, 'fsdp')
- vector_moments_new: float32 [2, 12, 768], P(None, None, 'fsdp')
The draws below stay inside these ranges and needn't reach their ends.
Inputs may be any that keep to these rules, and one draw needn't show every extreme that they name: `seq_lengths`: row s holds the lengths of the 8 sequences of device slice s; every row sums to 128 and its largest entry is 64. `wide_moments`: index 0 of the leading dimension holds first moments, index 1 second moments, which are positive. `proj_moments`: index 0 of the leading dimension holds first moments, index 1 second moments, which are positive. `vector_moments`: index 0 of the leading dimension holds first moments, index 1 second moments, which are positive.
All inputs are finite; a program needn't handle non-finite values.
Results may differ from the reference program's by a relative error of at most 0.012.
The reference program's roundings to bfloat16 on the way count: a program that leaves them out, or rounds other values in their place, can miss the bound.
Values may be sent and summed in bfloat16 or wider, within the bound.
A program may use at most 192 MiB of HBM per device.

```python
import math
import jax
import jax.numpy as jnp
import numpy as np
from jax import lax

D = 768
H = 12
HD = 64
FF = 3072
TOK_DEV = 128
SEQS_DEV = 8
STEP = 2
LMAX = 64
TOKENS = 4096
SLICES = 32
VROWS = 12
N_FSDP = 32


def draw_wide_weights(key, part):
    base_key = jax.random.fold_in(key, 0)
    standard = jax.random.normal(base_key, (D, 4 * D + FF), jnp.float32) / math.sqrt(D)
    column = jnp.arange(4 * D + FF)
    factor = jnp.where((column >= 3 * D) & (column < 4 * D), 4.0, 1.0)
    sampled = standard * factor[None, :]
    return jnp.clip(sampled, -2.0, 2.0)


def draw_vector_params(key, part):
    gain_key, shift_key = jax.random.split(key)
    row_index = jnp.arange(VROWS)[:, None]
    gains = jax.random.uniform(gain_key, (VROWS, D), jnp.float32, 0.5, 1.5)
    shifts = jnp.clip(0.3 * jax.random.normal(shift_key, (VROWS, D), jnp.float32), -1.0, 1.0)
    is_gain = (row_index == 0) | (row_index == 5)
    return jnp.where(is_gain, gains, shifts)


def draw_moment_pair(key, shape):
    first_key, second_key = jax.random.split(key)
    signed = jnp.clip(jax.random.normal(first_key, shape, jnp.float32), -4.0, 4.0) * 0.04
    log_low = math.log(0.0005)
    log_high = math.log(0.01)
    positive = jnp.exp(jax.random.uniform(second_key, shape, jnp.float32, log_low, log_high))
    return jnp.stack([signed, positive])


def draw_wide_moments(key, part):
    return draw_moment_pair(key, (D, 4 * D + FF))


def draw_proj_moments(key, part):
    return draw_moment_pair(key, (FF, D))


def draw_vector_moments(key, part):
    return draw_moment_pair(key, (VROWS, D))


def raised(array, rng, source, target, blocks, factor):
    owner, partner = [(jnp.arange(array.shape[dim]) // (array.shape[dim] // blocks)).reshape([-1 if axis == dim else 1 for axis in range(array.ndim)]) for dim in (source, target)]
    chosen = jax.random.permutation(rng, blocks)[partner]
    strong = (owner == chosen) | (owner == (partner + blocks // 2) % blocks)
    return jnp.where(strong, factor * array, array)


def block_levels(stream_key, shape, shards, least, top_value):
    def one(dim, blocks):
        draws = jax.random.uniform(jax.random.fold_in(jax.random.fold_in(stream_key, 6), dim), (blocks,), jnp.float32, least / len(shards), top_value / len(shards))
        return jnp.repeat(jnp.exp(draws), shape[dim] // blocks).reshape((-1,) + (1,) * (len(shape) - dim - 1))

    factor_of = one(*shards[0])
    for cut in shards[1:]:
        factor_of = factor_of * one(*cut)
    return factor_of


def length_profile(number_of, total, bound, slope):
    loads = [(1 << 20) // math.isqrt(grade ** slope) + 1 for grade in range(2, number_of + 1)]
    spare, counts = total - bound - (number_of - 1), [1] * (number_of - 1)
    while spare > 0:
        candidates = [i for i in range(number_of - 1) if counts[i] < bound]
        mass, remaining = sum([loads[i] for i in candidates]), spare
        for i in candidates:
            addition = min(bound - counts[i], max(1, remaining * loads[i] // mass), spare)
            counts[i] = counts[i] + addition
            spare = spare - addition
    return np.array([bound] + counts)


def uneven_parts(rng, number_of, total, bound, slope):
    if number_of == 2:
        one = jax.random.randint(rng, (), max(1, total - bound), min(bound, total - 1) + 1)
        return jnp.stack([one, total - one])
    sizes = jnp.asarray(length_profile(number_of, total, bound, slope), jnp.int32)
    couples = (number_of - 1) // 2
    giver, taker = sizes[1:1 + 2 * couples:2], sizes[2:2 + 2 * couples:2]
    room = jnp.minimum(giver - 1, bound - taker)
    shifted = jax.random.randint(jax.random.fold_in(rng, 1), (couples,), 0, 1 << 20) % (room + 1)
    sizes = sizes.at[1:1 + 2 * couples:2].set(giver - shifted).at[2:2 + 2 * couples:2].set(taker + shifted)
    return sizes[jax.random.permutation(jax.random.fold_in(rng, 2), number_of)]


def bell_draw(key, extent, spread, reach, cuts=(), kind=jnp.bfloat16):
    loudness = block_levels(key, extent, cuts, -0.22, 0.18) if cuts else 1.0
    entries = jax.random.normal(key, extent, jnp.float32) * spread * loudness
    return jnp.minimum(jnp.maximum(entries, -reach), reach).astype(kind)


def heavy_noise(stream_key, dims, width, most, cuts, heavy, held_as=jnp.bfloat16):
    array = width * jax.random.normal(stream_key, dims, jnp.float32)
    if cuts:
        array = array * block_levels(stream_key, dims, cuts, -0.22, 0.18)
    return jnp.clip(raised(array, jax.random.fold_in(stream_key, 3), *heavy), -most, most).astype(held_as)


def setup_inputs(seed: int = 0) -> dict:
    key_of = jax.random.split(jax.random.key(seed), 10)
    return {
        "tokens": bell_draw(key_of[0], (TOKENS, D), 1.0, 6.0, ((0, 32),)),
        "seq_lengths": jax.vmap(lambda own: uneven_parts(own, SEQS_DEV, TOK_DEV, LMAX, 2))(jax.random.split(key_of[1], SLICES)).reshape((SLICES, SEQS_DEV)).astype(jnp.int32),
        "cotangent": heavy_noise(key_of[2], (TOKENS, D), 1.0, 6.0, ((0, 32),), (0, 1, 32, 2.75)),
        "wide_weights": draw_wide_weights(jax.random.fold_in(key_of[9], 71), 0),
        "proj_weights": bell_draw(key_of[4], (FF, D), FF ** -0.5, 0.109375, ((0, 32),), jnp.float32),
        "vector_params": draw_vector_params(jax.random.fold_in(key_of[9], 71), 0),
        "wide_moments": draw_wide_moments(jax.random.fold_in(key_of[9], 71), 0),
        "proj_moments": draw_proj_moments(jax.random.fold_in(key_of[9], 71), 0),
        "vector_moments": draw_vector_moments(jax.random.fold_in(key_of[9], 71), 0),
    }


norm_eps = 1e-05
beta_one = 0.9
beta_two = 0.95
adam_eps = 1e-08
rate_matrix = 0.02
rate_vector = 0.2
weight_decay = 0.1
gelu_coeff = 0.7978845608028654
masked_score = -1e+30

def to_half(values):
    return lax.optimization_barrier(values.astype(jnp.bfloat16))

def norm_forward(values, gain_row, offset):
    center = values - lax.optimization_barrier(jnp.mean(values, axis=1, keepdims=True))
    variance = lax.optimization_barrier(jnp.mean(center * center, axis=1, keepdims=True))
    inverse = lax.rsqrt(variance + norm_eps)
    normed = center * inverse
    return (normed * gain_row + offset, normed, inverse)

def norm_backward(upstream, normed, inverse, gain_row):
    scaled = upstream * gain_row
    mean_term = lax.optimization_barrier(jnp.mean(scaled, axis=1, keepdims=True))
    proj_term = lax.optimization_barrier(jnp.mean(scaled * normed, axis=1, keepdims=True))
    input_grad = inverse * (scaled - mean_term - normed * proj_term)
    return (input_grad, lax.optimization_barrier(jnp.sum(upstream * normed, axis=0)), lax.optimization_barrier(jnp.sum(upstream, axis=0)))

def gelu_parts(before):
    inner_arg = gelu_coeff * (before + 0.044715 * before * before * before)
    tangent = jnp.tanh(inner_arg)
    value_part = 0.5 * before * (1.0 + tangent)
    slope_part = 0.5 * (1.0 + tangent) + 0.5 * before * (1.0 - tangent * tangent) * gelu_coeff * (1.0 + 3.0 * 0.044715 * before * before)
    return (value_part, slope_part)

def allowed_pairs(length_row, row_count):
    bounds = jnp.cumsum(length_row.astype(jnp.int32))
    position = jnp.arange(row_count, dtype=jnp.int32)
    segment = lax.optimization_barrier(jnp.sum((position[:, None] >= bounds[None, :]).astype(jnp.int32), axis=1))
    return (segment[:, None] == segment[None, :]) & (position[None, :] <= position[:, None])

def head_view(matrix):
    return matrix.astype(jnp.float32).reshape(matrix.shape[0], H, HD)

def score_table(queries, key_rows, allowed):
    scale_factor = 1.0 / math.sqrt(HD)
    scores = jnp.einsum('qhd,khd->hqk', head_view(queries), head_view(key_rows)) * scale_factor
    return jnp.where(allowed[None, :, :], scores, masked_score)

def attention_forward(queries, key_rows, value_rows, allowed):
    scores = score_table(queries, key_rows, allowed)
    highest = lax.optimization_barrier(jnp.max(scores, axis=2, keepdims=True))
    logsum = highest + jnp.log(lax.optimization_barrier(jnp.sum(jnp.exp(scores - highest), axis=2, keepdims=True)))
    weights = to_half(jnp.exp(scores - logsum)).astype(jnp.float32)
    mixed = jnp.einsum('hqk,khd->qhd', weights, head_view(value_rows))
    return (to_half(mixed.reshape(queries.shape[0], D)), logsum)

def attention_backward(queries, key_rows, value_rows, allowed, logsum, upstream):
    scale_factor = 1.0 / math.sqrt(HD)
    scores = score_table(queries, key_rows, allowed)
    probs = jnp.exp(scores - logsum)
    rounded = to_half(probs).astype(jnp.float32)
    grad_heads = head_view(upstream)
    value_grad = jnp.einsum('hqk,qhd->khd', rounded, grad_heads)
    prob_grad = jnp.einsum('qhd,khd->hqk', grad_heads, head_view(value_rows))
    delta_row = lax.optimization_barrier(jnp.sum(probs * prob_grad, axis=2, keepdims=True))
    score_grad = to_half(probs * (prob_grad - delta_row) * scale_factor).astype(jnp.float32)
    query_grad = jnp.einsum('hqk,khd->qhd', score_grad, head_view(key_rows))
    key_grad = jnp.einsum('hqk,qhd->khd', score_grad, head_view(queries))
    row_total = queries.shape[0]
    joined = jnp.concatenate([query_grad.reshape(row_total, D), key_grad.reshape(row_total, D), value_grad.reshape(row_total, D)], axis=1)
    return to_half(joined)

def slice_pass(token_rows, cot_rows, length_row, wide_half, proj_half, vector_half):
    vectors = vector_half.astype(jnp.float32)
    gain_one, shift_one, query_bias, value_bias = (vectors[0], vectors[1], vectors[2], vectors[3])
    out_bias, gain_two, shift_two, proj_bias = (vectors[4], vectors[5], vectors[6], vectors[7])
    fc_bias = vectors[8:].reshape(FF)
    qkv_weights = wide_half[:, :3 * D]
    out_weights = wide_half[:, 3 * D:4 * D]
    fc_weights = wide_half[:, 4 * D:]
    row_count = token_rows.shape[0]
    allowed = allowed_pairs(length_row, row_count)
    token_float = token_rows.astype(jnp.float32)
    first_norm, normed_one, inverse_one = norm_forward(token_float, gain_one, shift_one)
    first_in = to_half(first_norm)
    qkv_bias = jnp.concatenate([query_bias, jnp.zeros_like(query_bias), value_bias])
    qkv_half = to_half(jnp.dot(first_in, qkv_weights, preferred_element_type=jnp.float32) + qkv_bias)
    queries = qkv_half[:, :D]
    key_rows = qkv_half[:, D:2 * D]
    value_rows = qkv_half[:, 2 * D:]
    attended, logsum = attention_forward(queries, key_rows, value_rows, allowed)
    residual = token_float + jnp.dot(attended, out_weights, preferred_element_type=jnp.float32) + out_bias
    second_norm, normed_two, inverse_two = norm_forward(residual, gain_two, shift_two)
    second_in = to_half(second_norm)
    before_act = jnp.dot(second_in, fc_weights, preferred_element_type=jnp.float32) + fc_bias
    value_part, slope_part = gelu_parts(before_act)
    hidden = to_half(value_part)
    block_rows = (residual + jnp.dot(hidden, proj_half, preferred_element_type=jnp.float32) + proj_bias).astype(jnp.bfloat16)
    cot_float = cot_rows.astype(jnp.float32)
    proj_bias_grad = lax.optimization_barrier(jnp.sum(cot_float, axis=0))
    proj_grad = jnp.dot(hidden.T, cot_rows, preferred_element_type=jnp.float32)
    hidden_grad = jnp.dot(cot_rows, proj_half.T, preferred_element_type=jnp.float32)
    pre_grad = to_half(hidden_grad * slope_part)
    fc_bias_grad = lax.optimization_barrier(jnp.sum(pre_grad.astype(jnp.float32), axis=0))
    fc_grad = jnp.dot(second_in.T, pre_grad, preferred_element_type=jnp.float32)
    second_grad = jnp.dot(pre_grad, fc_weights.T, preferred_element_type=jnp.float32)
    resid_norm_grad, gain_two_grad, shift_two_grad = norm_backward(second_grad, normed_two, inverse_two, gain_two)
    resid_grad = cot_float + resid_norm_grad
    resid_half = to_half(resid_grad)
    out_bias_grad = lax.optimization_barrier(jnp.sum(resid_grad, axis=0))
    out_grad = jnp.dot(attended.T, resid_half, preferred_element_type=jnp.float32)
    attended_grad = to_half(jnp.dot(resid_half, out_weights.T, preferred_element_type=jnp.float32))
    qkv_grad = attention_backward(queries, key_rows, value_rows, allowed, logsum, attended_grad)
    query_bias_grad = lax.optimization_barrier(jnp.sum(qkv_grad[:, :D].astype(jnp.float32), axis=0))
    value_bias_grad = lax.optimization_barrier(jnp.sum(qkv_grad[:, 2 * D:].astype(jnp.float32), axis=0))
    qkv_weight_grad = jnp.dot(first_in.T, qkv_grad, preferred_element_type=jnp.float32)
    first_grad = jnp.dot(qkv_grad, qkv_weights.T, preferred_element_type=jnp.float32)
    token_norm_grad, gain_one_grad, shift_one_grad = norm_backward(first_grad, normed_one, inverse_one, gain_one)
    token_grad_rows = (resid_grad + token_norm_grad).astype(jnp.bfloat16)
    wide_part = jnp.concatenate([qkv_weight_grad, out_grad, fc_grad], axis=1)
    vector_part = jnp.concatenate([jnp.stack([gain_one_grad, shift_one_grad, query_bias_grad, value_bias_grad, out_bias_grad, gain_two_grad, shift_two_grad, proj_bias_grad]), fc_bias_grad.reshape(FF // D, D)], axis=0)
    return (block_rows, token_grad_rows, wide_part, proj_grad, vector_part)

def adam_update(weights, moments, gradient, rate, decay_rate, unscale):
    scaled_grad = gradient / unscale
    first_moment = beta_one * moments[0] + (1.0 - beta_one) * scaled_grad
    second_moment = beta_two * moments[1] + (1.0 - beta_two) * scaled_grad * scaled_grad
    corrected_first = first_moment / (1.0 - beta_one ** STEP)
    corrected_second = second_moment / (1.0 - beta_two ** STEP)
    updated = weights - rate * (corrected_first / (jnp.sqrt(corrected_second) + adam_eps) + decay_rate * weights)
    return (updated, jnp.stack([first_moment, second_moment]))

def reference(tokens, seq_lengths, cotangent, wide_weights, proj_weights, vector_params, wide_moments, proj_moments, vector_moments):
    wide_half = to_half(wide_weights)
    proj_half = to_half(proj_weights)
    vector_half = to_half(vector_params)

    def one_slice(carry, inputs):
        token_rows, cot_rows, length_row = inputs
        block_rows, token_grad_rows, wide_part, proj_part, vector_part = slice_pass(token_rows, cot_rows, length_row, wide_half, proj_half, vector_half)
        carry_next = (carry[0] + wide_part, carry[1] + proj_part, carry[2] + vector_part)
        return (carry_next, (block_rows, token_grad_rows))
    start_sums = (jnp.zeros((D, 4 * D + FF), jnp.float32), jnp.zeros((FF, D), jnp.float32), jnp.zeros((8 + FF // D, D), jnp.float32))
    sliced = (tokens.reshape(N_FSDP, TOK_DEV, D), cotangent.reshape(N_FSDP, TOK_DEV, D), seq_lengths)
    sums, (block_all, grad_all) = lax.scan(one_slice, start_sums, sliced)
    wide_grad, proj_grad, vector_grad = sums
    unscale = math.sqrt(N_FSDP * TOK_DEV)
    wide_new, wide_moments_new = adam_update(wide_weights, wide_moments, wide_grad, rate_matrix, weight_decay, unscale)
    proj_new, proj_moments_new = adam_update(proj_weights, proj_moments, proj_grad, rate_matrix, weight_decay, unscale)
    vector_new, vector_moments_new = adam_update(vector_params, vector_moments, vector_grad, rate_vector, 0.0, unscale)
    block_output = block_all.reshape(N_FSDP * TOK_DEV, D)
    tokens_grad = grad_all.reshape(N_FSDP * TOK_DEV, D)
    return (block_output, tokens_grad, wide_grad, proj_grad, vector_grad, wide_new, proj_new, vector_new, wide_moments_new, proj_moments_new, vector_moments_new)
```

```python
import functools
import math

import jax
import jax.numpy as jnp
from jax import lax
from jax.experimental import pallas as pl
from jax.experimental.pallas import tpu as pltpu
from jax.sharding import PartitionSpec as P

D = 768
H = 12
HD = 64
FF = 3072
STEP = 2


norm_eps = 1e-05
beta_one = 0.9
beta_two = 0.95
adam_eps = 1e-08
rate_matrix = 0.02
rate_vector = 0.2
weight_decay = 0.1
gelu_coeff = 0.7978845608028654
masked_score = -1e30


def norm_forward(values, gain_row, offset):
    center = values - jnp.mean(values, axis=1, keepdims=True)
    variance = jnp.mean(center * center, axis=1, keepdims=True)
    inverse = lax.rsqrt(variance + norm_eps)
    normed = center * inverse
    return (normed * gain_row + offset, normed, inverse)


def norm_backward(upstream, normed, inverse, gain_row):
    scaled = upstream * gain_row
    mean_term = jnp.mean(scaled, axis=1, keepdims=True)
    proj_term = jnp.mean(scaled * normed, axis=1, keepdims=True)
    input_grad = inverse * (scaled - mean_term - normed * proj_term)
    return (input_grad, jnp.sum(upstream * normed, axis=0), jnp.sum(upstream, axis=0))


def gelu_parts(before):
    inner_arg = gelu_coeff * (before + 0.044715 * before * before * before)
    tangent = jnp.tanh(inner_arg)
    value_part = 0.5 * before * (1.0 + tangent)
    slope_part = 0.5 * (1.0 + tangent) + 0.5 * before * (1.0 - tangent * tangent) * gelu_coeff * (
        1.0 + 3.0 * 0.044715 * before * before
    )
    return (value_part, slope_part)


def allowed_pairs(length_row, row_count):
    bounds = jnp.cumsum(length_row)
    position = jnp.arange(row_count, dtype=jnp.int32)
    segment = jnp.sum((position[:, None] >= bounds[None, :]).astype(jnp.int32), axis=1)
    return (segment[:, None] == segment[None, :]) & (position[None, :] <= position[:, None])


def head_view(matrix):
    return matrix.reshape(matrix.shape[0], H, HD)


def score_table(queries, key_rows, allowed):
    scale_factor = 1.0 / math.sqrt(HD)
    scores = (
        jnp.einsum(
            "qhd,khd->hqk",
            head_view(queries),
            head_view(key_rows),
            preferred_element_type=jnp.float32,
        )
        * scale_factor
    )
    return jnp.where(allowed[None, :, :], scores, masked_score)


def attention_forward(queries, key_rows, value_rows, allowed):
    scores = score_table(queries, key_rows, allowed)
    highest = jnp.max(scores, axis=2, keepdims=True)
    logsum = highest + jnp.log(jnp.sum(jnp.exp(scores - highest), axis=2, keepdims=True))
    weights = jnp.exp(scores - logsum).astype(jnp.bfloat16)
    mixed = jnp.einsum(
        "hqk,khd->qhd", weights, head_view(value_rows), preferred_element_type=jnp.float32
    )
    return (mixed.reshape(queries.shape[0], D).astype(jnp.bfloat16), logsum)


def attention_backward(queries, key_rows, value_rows, allowed, logsum, upstream):
    scale_factor = 1.0 / math.sqrt(HD)
    scores = score_table(queries, key_rows, allowed)
    probs = jnp.exp(scores - logsum)
    rounded = probs.astype(jnp.bfloat16)
    grad_heads = head_view(upstream)
    value_grad = jnp.einsum("hqk,qhd->khd", rounded, grad_heads, preferred_element_type=jnp.float32)
    prob_grad = jnp.einsum(
        "qhd,khd->hqk", grad_heads, head_view(value_rows), preferred_element_type=jnp.float32
    )
    delta_row = jnp.sum(probs * prob_grad, axis=2, keepdims=True)
    score_grad = (probs * (prob_grad - delta_row) * scale_factor).astype(jnp.bfloat16)
    query_grad = jnp.einsum(
        "hqk,khd->qhd", score_grad, head_view(key_rows), preferred_element_type=jnp.float32
    )
    key_grad = jnp.einsum(
        "hqk,qhd->khd", score_grad, head_view(queries), preferred_element_type=jnp.float32
    )
    row_total = queries.shape[0]
    joined = jnp.concatenate(
        [
            query_grad.reshape(row_total, D),
            key_grad.reshape(row_total, D),
            value_grad.reshape(row_total, D),
        ],
        axis=1,
    )
    return joined.astype(jnp.bfloat16)


def adam_update(weights, moments, gradient, rate, decay_rate, unscale):
    scaled_grad = gradient / unscale
    first_moment = beta_one * moments[0] + (1.0 - beta_one) * scaled_grad
    second_moment = beta_two * moments[1] + (1.0 - beta_two) * scaled_grad * scaled_grad
    corrected_first = first_moment / (1.0 - beta_one**STEP)
    corrected_second = second_moment / (1.0 - beta_two**STEP)
    updated = weights - rate * (
        corrected_first / (jnp.sqrt(corrected_second) + adam_eps) + decay_rate * weights
    )
    return (updated, jnp.stack([first_moment, second_moment]))


def column_term(left, right):
    return jnp.einsum("tc,te->ce", left, right, preferred_element_type=jnp.float32)


MESH = pl.DeviceIdType.MESH
WIDE_A = 6 * D
GROUP = 24


def position(n):
    depth = n // 8
    me = lax.axis_index("fsdp")
    return depth, me // 8, (me // 4) % 2, (me // 2) % 2, me % 2


def device_at(z, y, x, c):
    return ((z * 2 + y) * 2 + x) * 2 + c


def greet(partners):
    barrier = pltpu.get_barrier_semaphore()
    for device in partners:
        pl.semaphore_signal(barrier, inc=1, device_id=(device,), device_id_type=MESH)
    pl.semaphore_wait(barrier, len(partners))


def remote(src, dst, send, recv, device):
    return pltpu.make_async_remote_copy(
        src_ref=src,
        dst_ref=dst,
        send_sem=send,
        recv_sem=recv,
        device_id=(device,),
        device_id_type=MESH,
    )


def gather_kernel(n, wide, proj, vec, wide_out, proj_out, vec_out, local, ssem, rsem):
    depth, z, y, x, c = position(n)
    z_peers = [device_at((z + d) % depth, y, x, c) for d in range(1, depth)]
    y_peer, x_peer = device_at(z, 1 - y, x, c), device_at(z, y, 1 - x, c)
    core_peer = device_at(z, y, x, 1 - c)
    greet(z_peers + [y_peer, x_peer, core_peer])
    sends = []
    count = [0]

    def push(src, dst, device, landed):
        k = count[0]
        count[0] = k + 1
        copy = remote(src, dst, ssem.at[k], rsem.at[k], device)
        copy.start()
        sends.append(copy)
        return remote(landed, landed, ssem.at[k], rsem.at[k], device)

    own = [
        pltpu.make_async_copy(wide, wide_out.at[z, y, x, c], local.at[0]),
        pltpu.make_async_copy(proj, proj_out.at[z, y, x, c], local.at[1]),
        pltpu.make_async_copy(vec, vec_out.at[z, y, x, c], local.at[2]),
    ]
    for copy in own:
        copy.start()

    def wide_low(zi, p, q, ci):
        return wide_out.at[zi, p, q, ci, :, pl.ds(0, WIDE_A)]

    def wide_high(zi, p, q, ci):
        return wide_out.at[zi, q, p, ci, :, pl.ds(WIDE_A, wide.shape[1] - WIDE_A)]

    def proj_at(zi, p, q, ci):
        return proj_out.at[zi, q, p, ci]

    def vec_at(zi, p, q, ci):
        return vec_out.at[zi, q, p, ci]

    yx = (y, x, y_peer, x_peer)
    xy = (x, y, x_peer, y_peer)
    streams = [
        (wide.at[:, pl.ds(0, WIDE_A)], wide_low, yx),
        (wide.at[:, pl.ds(WIDE_A, wide.shape[1] - WIDE_A)], wide_high, xy),
        (proj, proj_at, xy),
        (vec, vec_at, xy),
    ]
    every = pl.ds(0, depth)
    from_z = [[] for _ in streams]
    from_first = [[] for _ in streams]
    from_second = [[] for _ in streams]
    from_far = [[] for _ in streams]
    from_core = []
    for d in range(1, depth):
        for s, (mine, at, (p, q, _, _)) in enumerate(streams):
            from_z[s].append(
                push(mine, at(z, p, q, c), z_peers[d - 1], at((z + depth - d) % depth, p, q, c))
            )
    for s, (mine, at, (p, q, first, second)) in enumerate(streams):
        from_first[s].append(push(mine, at(z, p, q, c), first, at(z, 1 - p, q, c)))
        from_second[s].append(push(mine, at(z, p, q, c), second, at(z, p, 1 - q, c)))
    for copy in own:
        copy.wait()
    for d in range(1, depth):
        zi = (z + depth - d) % depth
        for s, (mine, at, (p, q, first, second)) in enumerate(streams):
            from_z[s][d - 1].wait_recv()
            here = at(zi, p, q, c)
            from_first[s].append(push(here, here, first, at(zi, 1 - p, q, c)))
            from_second[s].append(push(here, here, second, at(zi, p, 1 - q, c)))
    for mine, at, (p, q, _, _) in streams:
        here = at(every, p, q, c)
        from_core.append(push(here, here, core_peer, at(every, p, q, 1 - c)))
    for d in range(depth):
        zi = (z + depth - d) % depth
        for s, (mine, at, (p, q, first, second)) in enumerate(streams):
            from_first[s][d].wait_recv()
            here = at(zi, 1 - p, q, c)
            from_far[s].append(push(here, here, second, at(zi, 1 - p, 1 - q, c)))
    for mine, at, (p, q, _, _) in streams:
        here = at(every, 1 - p, q, c)
        from_core.append(push(here, here, core_peer, at(every, 1 - p, q, 1 - c)))
    for s, (mine, at, (p, q, _, _)) in enumerate(streams):
        for d in range(depth):
            from_second[s][d].wait_recv()
        here = at(every, p, 1 - q, c)
        from_core.append(push(here, here, core_peer, at(every, p, 1 - q, 1 - c)))
    for s, (mine, at, (p, q, _, _)) in enumerate(streams):
        for d in range(depth):
            from_far[s][d].wait_recv()
        here = at(every, 1 - p, 1 - q, c)
        from_core.append(push(here, here, core_peer, at(every, 1 - p, 1 - q, 1 - c)))
    for copy in from_core:
        copy.wait_recv()
    for copy in sends:
        copy.wait_send()


def gather_all(n, wide, proj, vec):
    depth = n // 8
    lead = (depth, 2, 2, 2)
    copies = 4 * (depth - 1 + 3 * depth + 4)
    out = tuple(jax.ShapeDtypeStruct(lead + part.shape, part.dtype) for part in (wide, proj, vec))
    space = pl.BlockSpec(memory_space=pl.ANY)
    wide_out, proj_out, vec_out = pl.pallas_call(
        functools.partial(gather_kernel, n),
        out_shape=out,
        in_specs=[space] * 3,
        out_specs=(space,) * 3,
        scratch_shapes=[
            pltpu.SemaphoreType.DMA((3,)),
            pltpu.SemaphoreType.DMA((copies,)),
            pltpu.SemaphoreType.DMA((copies,)),
        ],
        compiler_params=pltpu.CompilerParams(collective_id=0, has_side_effects=True),
    )(wide, proj, vec)
    return (
        wide_out.reshape(n * wide.shape[0], wide.shape[1]),
        proj_out.reshape(n * proj.shape[0], proj.shape[1]),
        vec_out.reshape(n, *vec.shape),
    )


def scatter_kernel(
    n,
    in_a,
    att_a,
    sec_a,
    sec_b,
    hid_b,
    qkv_g,
    res_g,
    pre_g,
    cot,
    vec,
    wide_out,
    proj_out,
    vec_out,
    given,
    kept,
    land_core,
    land_second,
    land_third,
    land_z,
    vec_kept,
    vec_core,
    vec_second,
    vec_third,
    vec_z,
    ssem,
    rsem,
):
    depth, z, y, x, c = position(n)
    z_devices = [device_at((z + d) % depth, y, x, c) for d in range(1, depth)]
    y_peer, x_peer = device_at(z, 1 - y, x, c), device_at(z, y, 1 - x, c)
    core_peer = device_at(z, y, x, 1 - c)
    greet(z_devices + [y_peer, x_peer, core_peer])
    second_peer = (x_peer, y_peer)
    third_peer = (y_peer, x_peer)
    spots = ((x, y), (y, x))
    sends = []
    count = [8]

    def push(src, dst, device):
        k = count[0]
        count[0] = k + 1
        copy = remote(src, dst, ssem.at[k], rsem.at[k], device)
        copy.start()
        sends.append(copy)
        return copy

    vec_copy = push(vec.at[1 - c], vec_core, core_peer)

    def product(left, right):
        return jnp.dot(left, right, preferred_element_type=jnp.float32)

    def block(left, right):
        return product(left, right).reshape(depth, GROUP, D)

    def fill(s, half, t, target):
        i = (spots[s][0] + 1 - t // 2) % 2
        j = (spots[s][1] + 1 - t % 2) % 2
        if s == 0:
            left = in_a[half, i, j]
            target[:, 0:48, :] = jnp.concatenate(
                [block(left, qkv_g[:, 0:D]), block(left, qkv_g[:, D : 2 * D])], axis=1
            ).astype(jnp.bfloat16)
            target[:, 48:96, :] = jnp.concatenate(
                [
                    block(left, qkv_g[:, 2 * D : 3 * D]),
                    block(att_a[half, i, j], res_g[...]),
                ],
                axis=1,
            ).astype(jnp.bfloat16)
            left = sec_a[half, i, j]
            target[:, 96:144, :] = jnp.concatenate(
                [block(left, pre_g[:, 0:D]), block(left, pre_g[:, D : 2 * D])], axis=1
            ).astype(jnp.bfloat16)
        else:
            left = sec_b[half, i, j]
            target[:, 0:48, :] = jnp.concatenate(
                [block(left, pre_g[:, 2 * D : 3 * D]), block(left, pre_g[:, 3 * D : 4 * D])],
                axis=1,
            ).astype(jnp.bfloat16)
            target[:, 48:144, :] = (
                product(hid_b[half, i, j], cot[...]).reshape(depth, 96, D).astype(jnp.bfloat16)
            )

    def core_copy(s, t):
        k = s * 4 + t
        return remote(given.at[s, t], land_core.at[s, t], ssem.at[k], rsem.at[k], core_peer)

    def give(t, carry):
        for s in range(2):
            fill(s, 1 - c, t, given.at[s, t])
            core_copy(s, t).start()
        return carry

    lax.fori_loop(0, 4, give, 0)

    def keep(t, carry):
        for s in range(2):
            fill(s, c, t, kept.at[s, t])
        return carry

    lax.fori_loop(0, 4, keep, 0)

    def merge(target, landed):
        def step(k, carry):
            target[k] = (
                target[k].astype(jnp.float32) + landed[k].astype(jnp.float32)
            ).astype(jnp.bfloat16)
            return carry

        lax.fori_loop(0, depth, step, 0)

    vec_copy.wait_recv()
    vec_kept[...] = vec[c] + vec_core[...]
    vec_copy = push(vec_kept.at[1 - x], vec_second, x_peer)
    second = [[], []]
    for t in range(2):
        for s in range(2):
            core_copy(s, t).wait_recv()
            merge(kept.at[s, t], land_core.at[s, t])
            second[s].append(push(kept.at[s, t], land_second.at[s, t], second_peer[s]))
    for t in range(2, 4):
        for s in range(2):
            core_copy(s, t).wait_recv()
            merge(kept.at[s, t], land_core.at[s, t])
    vec_copy.wait_recv()
    vec_kept[x] += vec_second[...]
    vec_copy = push(vec_kept.at[x, 1 - y], vec_third, y_peer)
    third = []
    for s in range(2):
        second[s][0].wait_recv()
        merge(kept.at[s, 2], land_second.at[s, 0])
        third.append(push(kept.at[s, 2], land_third.at[s], third_peer[s]))
    for s in range(2):
        second[s][1].wait_recv()
        merge(kept.at[s, 3], land_second.at[s, 1])
    vec_copy.wait_recv()
    vec_kept[x, y] += vec_third[...]
    vec_last = [
        push(vec_kept.at[x, y, (z + d) % depth], vec_z.at[d - 1], z_devices[d - 1])
        for d in range(1, depth)
    ]
    last = [[], []]
    for s in range(2):
        third[s].wait_recv()
        merge(kept.at[s, 3], land_third.at[s])
        for d in range(1, depth):
            last[s].append(
                push(kept.at[s, 3, (z + d) % depth], land_z.at[s, d - 1], z_devices[d - 1])
            )
    total = vec_kept[x, y, z]
    for d in range(depth - 1):
        vec_last[d].wait_recv()
        total += vec_z[d]
    vec_out[...] = total
    for s in range(2):
        for d in range(depth - 1):
            last[s][d].wait_recv()
        total = kept[s, 3, z].astype(jnp.float32)
        for d in range(depth - 1):
            total += land_z[s, d].astype(jnp.float32)
        if s == 0:
            for b in range(6):
                wide_out[:, b * D : (b + 1) * D] = total[b * GROUP : (b + 1) * GROUP]
        else:
            for b in range(2):
                wide_out[:, (6 + b) * D : (7 + b) * D] = total[b * GROUP : (b + 1) * GROUP]
            proj_out[...] = total[2 * GROUP :]
    for s in range(2):
        for t in range(4):
            core_copy(s, t).wait_send()
    for copy in sends:
        copy.wait_send()


def by_owner(rows, n, order):
    depth = n // 8
    size = rows.shape[0] // n
    names = {"y": 1, "x": 2, "c": 3}
    split = rows.reshape(depth, 2, 2, 2, size, *rows.shape[1:])
    rest = tuple(range(4, split.ndim))
    return split.transpose(*(names[k] for k in order), 0, *rest)


def scatter_all(n, first_in, attended, second_in, hidden, qkv_grad, resid_half, pre_grad, cot, vec):
    depth = n // 8

    def left(rows, order):
        ordered = by_owner(rows.T, n, order)
        return ordered.reshape(2, 2, 2, -1, rows.shape[0])

    dtype = jnp.bfloat16
    unit = (depth, 6 * GROUP, D)
    tile = vec.shape[1:]
    copies = 8 + 2 * (2 + 1 + depth - 1) + 3 + depth - 1
    space = pl.BlockSpec(memory_space=pltpu.VMEM)
    return pl.pallas_call(
        functools.partial(scatter_kernel, n),
        out_shape=(
            jax.ShapeDtypeStruct((GROUP, 8 * D), jnp.float32),
            jax.ShapeDtypeStruct((4 * GROUP, D), jnp.float32),
            jax.ShapeDtypeStruct(tile, jnp.float32),
        ),
        in_specs=[space] * 10,
        out_specs=(space,) * 3,
        scratch_shapes=[
            pltpu.VMEM((2, 4) + unit, dtype),
            pltpu.VMEM((2, 4) + unit, dtype),
            pltpu.VMEM((2, 4) + unit, dtype),
            pltpu.VMEM((2, 2) + unit, dtype),
            pltpu.VMEM((2,) + unit, dtype),
            pltpu.VMEM((2, depth - 1, 6 * GROUP, D), dtype),
            pltpu.VMEM((2, 2, depth) + tile, jnp.float32),
            pltpu.VMEM((2, 2, depth) + tile, jnp.float32),
            pltpu.VMEM((2, depth) + tile, jnp.float32),
            pltpu.VMEM((depth,) + tile, jnp.float32),
            pltpu.VMEM((depth - 1,) + tile, jnp.float32),
            pltpu.SemaphoreType.DMA((copies,)),
            pltpu.SemaphoreType.DMA((copies,)),
        ],
        compiler_params=pltpu.CompilerParams(
            collective_id=1, has_side_effects=True, vmem_limit_bytes=52 * 2**20
        ),
    )(
        left(first_in, "cxy"),
        left(attended, "cxy"),
        left(second_in, "cxy"),
        left(second_in, "cyx"),
        left(hidden, "cyx"),
        qkv_grad,
        resid_half,
        pre_grad,
        cot,
        by_owner(vec, n, "cxy").reshape(2, 2, 2, depth, *tile),
    )


def to_tile(rows):
    flat = rows.reshape(rows.shape[0], -1)
    return jnp.pad(flat, ((0, 0), (0, 1024 - flat.shape[1]))).reshape(rows.shape[0], 8, 128)


def from_tile(tiles, rows, columns):
    return tiles.reshape(tiles.shape[0], 1024)[:, : rows * columns].reshape(-1, rows, columns)


def body(
    tokens,
    seq_lengths,
    cotangent,
    wide_weights,
    proj_weights,
    vector_params,
    wide_moments,
    proj_moments,
    vector_moments,
):
    shards = (
        wide_weights.astype(jnp.bfloat16),
        proj_weights.astype(jnp.bfloat16),
        vector_params.astype(jnp.bfloat16),
    )
    devices = lax.axis_size("fsdp")
    direct = wide_weights.shape[0] == GROUP and devices % 8 == 0
    vector_rows, vector_columns = vector_params.shape
    if direct:
        wide_full, proj_full, vector_tiles = gather_all(
            devices, shards[0], shards[1], to_tile(shards[2].astype(jnp.float32)[None])[0]
        )
        vector_full = (
            from_tile(vector_tiles, vector_rows, vector_columns)
            .transpose(1, 0, 2)
            .reshape(vector_rows, devices * vector_columns)
        )
    else:
        wide_full, proj_full, vector_full = (
            lax.all_gather(shards[0], "fsdp", axis=0, tiled=True),
            lax.all_gather(shards[1], "fsdp", axis=0, tiled=True),
            lax.all_gather(shards[2], "fsdp", axis=1, tiled=True),
        )
    vectors = vector_full.astype(jnp.float32)
    row_count = tokens.shape[0]
    allowed = allowed_pairs(seq_lengths[0], row_count)
    ratio = FF // D
    local_rows = wide_weights.shape[0]
    unscale = math.sqrt(lax.axis_size("fsdp") * row_count)
    gain_one, shift_one, query_bias, value_bias = (vectors[0], vectors[1], vectors[2], vectors[3])
    out_bias, gain_two, shift_two, proj_bias = (vectors[4], vectors[5], vectors[6], vectors[7])
    fc_bias = vectors[8:].reshape(FF)
    token_float = tokens.astype(jnp.float32)
    first_norm, normed_one, inverse_one = norm_forward(token_float, gain_one, shift_one)
    first_in = first_norm.astype(jnp.bfloat16)
    qkv_bias = jnp.concatenate([query_bias, jnp.zeros_like(query_bias), value_bias])
    qkv_half = (
        jnp.dot(first_in, wide_full[:, : 3 * D], preferred_element_type=jnp.float32) + qkv_bias
    ).astype(jnp.bfloat16)
    queries = qkv_half[:, :D]
    key_rows = qkv_half[:, D : 2 * D]
    value_rows = qkv_half[:, 2 * D :]
    attended, logsum = attention_forward(queries, key_rows, value_rows, allowed)
    residual = (
        token_float
        + jnp.dot(attended, wide_full[:, 3 * D : 4 * D], preferred_element_type=jnp.float32)
        + out_bias
    )
    second_norm, normed_two, inverse_two = norm_forward(residual, gain_two, shift_two)
    second_in = second_norm.astype(jnp.bfloat16)
    before_act = (
        jnp.dot(second_in, wide_full[:, 4 * D :], preferred_element_type=jnp.float32) + fc_bias
    )
    value_part, slope_part = gelu_parts(before_act)
    hidden = value_part.astype(jnp.bfloat16)
    block_output = (
        residual + jnp.dot(hidden, proj_full, preferred_element_type=jnp.float32) + proj_bias
    ).astype(jnp.bfloat16)
    backward_wide, backward_proj, vector_again = wide_full, proj_full, vector_full
    backward_vectors = vector_again.astype(jnp.float32)
    qkv_back = backward_wide[:, : 3 * D]
    out_back = backward_wide[:, 3 * D : 4 * D]
    fc_back = backward_wide[:, 4 * D :]
    cot_float = cotangent.astype(jnp.float32)
    proj_bias_grad = jnp.sum(cot_float, axis=0)
    hidden_grad = jnp.einsum(
        "td,fd->tf", cotangent, backward_proj, preferred_element_type=jnp.float32
    )
    pre_grad = (hidden_grad * slope_part).astype(jnp.bfloat16)
    fc_bias_grad = jnp.sum(pre_grad, axis=0, dtype=jnp.float32)
    second_grad = jnp.einsum("tf,df->td", pre_grad, fc_back, preferred_element_type=jnp.float32)
    resid_norm_grad, gain_two_grad, shift_two_grad = norm_backward(
        second_grad, normed_two, inverse_two, backward_vectors[5]
    )
    resid_grad = cot_float + resid_norm_grad
    mlp_vectors = jnp.concatenate(
        [
            jnp.stack([gain_two_grad, shift_two_grad, proj_bias_grad]),
            fc_bias_grad.reshape(ratio, D),
        ],
        axis=0,
    )
    resid_half = resid_grad.astype(jnp.bfloat16)
    out_bias_grad = jnp.sum(resid_grad, axis=0)
    attended_grad = jnp.einsum(
        "te,de->td", resid_half, out_back, preferred_element_type=jnp.float32
    ).astype(jnp.bfloat16)
    qkv_grad = attention_backward(queries, key_rows, value_rows, allowed, logsum, attended_grad)
    query_bias_grad = jnp.sum(qkv_grad[:, :D], axis=0, dtype=jnp.float32)
    value_bias_grad = jnp.sum(qkv_grad[:, 2 * D :], axis=0, dtype=jnp.float32)
    first_grad = jnp.einsum("tc,dc->td", qkv_grad, qkv_back, preferred_element_type=jnp.float32)
    token_norm_grad, gain_one_grad, shift_one_grad = norm_backward(
        first_grad, normed_one, inverse_one, backward_vectors[0]
    )
    tokens_grad = (resid_grad + token_norm_grad).astype(jnp.bfloat16)
    attn_vectors = jnp.stack(
        [gain_one_grad, shift_one_grad, query_bias_grad, value_bias_grad, out_bias_grad]
    )
    vector_terms = jnp.concatenate([attn_vectors, mlp_vectors], axis=0)
    if direct:
        owned = vector_terms.reshape(vector_rows, devices, vector_columns).transpose(1, 0, 2)
        wide_grad, proj_grad, vector_tile = scatter_all(
            devices,
            first_in,
            attended,
            second_in,
            hidden,
            qkv_grad,
            resid_half,
            pre_grad,
            cotangent,
            to_tile(owned),
        )
        vector_grad = from_tile(vector_tile[None], vector_rows, vector_columns)[0]
    else:
        fc_part = column_term(second_in, pre_grad)
        proj_part = column_term(hidden, cotangent).reshape(
            local_rows * lax.axis_size("fsdp"), ratio * D
        )
        qkv_part = column_term(first_in, qkv_grad)
        out_part = column_term(attended, resid_half)
        joined_shard = lax.psum_scatter(
            jnp.concatenate(
                [
                    jnp.concatenate([qkv_part, out_part], axis=1),
                    jnp.concatenate([fc_part, proj_part], axis=1),
                ],
                axis=1,
            ),
            "fsdp",
            scatter_dimension=0,
            tiled=True,
        )
        wide_grad = joined_shard[:, : 4 * D + FF]
        proj_grad = joined_shard[:, 4 * D + FF :].reshape(local_rows * ratio, D)
        vector_grad = lax.psum_scatter(vector_terms, "fsdp", scatter_dimension=1, tiled=True)
    wide_new, wide_moments_new = adam_update(
        wide_weights, wide_moments, wide_grad, rate_matrix, weight_decay, unscale
    )
    proj_new, proj_moments_new = adam_update(
        proj_weights, proj_moments, proj_grad, rate_matrix, weight_decay, unscale
    )
    vector_new, vector_moments_new = adam_update(
        vector_params, vector_moments, vector_grad, rate_vector, 0.0, unscale
    )
    return (
        block_output,
        tokens_grad,
        wide_grad,
        proj_grad,
        vector_grad,
        wide_new,
        proj_new,
        vector_new,
        wide_moments_new,
        proj_moments_new,
        vector_moments_new,
    )


def solution(mesh):
    placed = (
        P("fsdp", None),
        P("fsdp", None),
        P("fsdp", None),
        P("fsdp", None),
        P("fsdp", None),
        P(None, "fsdp"),
        P(None, "fsdp", None),
        P(None, "fsdp", None),
        P(None, None, "fsdp"),
    )
    return jax.shard_map(
        body,
        mesh=mesh,
        in_specs=placed,
        out_specs=(
            P("fsdp", None),
            P("fsdp", None),
            P("fsdp", None),
            P("fsdp", None),
            P(None, "fsdp"),
            P("fsdp", None),
            P("fsdp", None),
            P(None, "fsdp"),
            P(None, "fsdp", None),
            P(None, "fsdp", None),
            P(None, None, "fsdp"),
        ),
        check_vma=False,
    )
```

```python
import functools
import math

import jax
import jax.numpy as jnp
from jax import lax
from jax.experimental import pallas as pl
from jax.experimental.pallas import tpu as pltpu
from jax.sharding import PartitionSpec as P

D = 768
H = 12
HD = 64
FF = 3072
STEP = 2


norm_eps = 1e-05
beta_one = 0.9
beta_two = 0.95
adam_eps = 1e-08
rate_matrix = 0.02
rate_vector = 0.2
weight_decay = 0.1
gelu_coeff = 0.7978845608028654
masked_score = -1e30


def norm_forward(values, gain_row, offset):
    center = values - jnp.mean(values, axis=1, keepdims=True)
    variance = jnp.mean(center * center, axis=1, keepdims=True)
    inverse = lax.rsqrt(variance + norm_eps)
    normed = center * inverse
    return (normed * gain_row + offset, normed, inverse)


def norm_backward(upstream, normed, inverse, gain_row):
    scaled = upstream * gain_row
    mean_term = jnp.mean(scaled, axis=1, keepdims=True)
    proj_term = jnp.mean(scaled * normed, axis=1, keepdims=True)
    input_grad = inverse * (scaled - mean_term - normed * proj_term)
    return (input_grad, jnp.sum(upstream * normed, axis=0), jnp.sum(upstream, axis=0))


def gelu_parts(before):
    inner_arg = gelu_coeff * (before + 0.044715 * before * before * before)
    tangent = jnp.tanh(inner_arg)
    value_part = 0.5 * before * (1.0 + tangent)
    slope_part = 0.5 * (1.0 + tangent) + 0.5 * before * (1.0 - tangent * tangent) * gelu_coeff * (
        1.0 + 3.0 * 0.044715 * before * before
    )
    return (value_part, slope_part)


def allowed_pairs(length_row, row_count):
    bounds = jnp.cumsum(length_row)
    position = jnp.arange(row_count, dtype=jnp.int32)
    segment = jnp.sum((position[:, None] >= bounds[None, :]).astype(jnp.int32), axis=1)
    return (segment[:, None] == segment[None, :]) & (position[None, :] <= position[:, None])


def head_view(matrix):
    return matrix.reshape(matrix.shape[0], H, HD)


def score_table(queries, key_rows, allowed):
    scale_factor = 1.0 / math.sqrt(HD)
    scores = (
        jnp.einsum(
            "qhd,khd->hqk",
            head_view(queries),
            head_view(key_rows),
            preferred_element_type=jnp.float32,
        )
        * scale_factor
    )
    return jnp.where(allowed[None, :, :], scores, masked_score)


def attention_forward(queries, key_rows, value_rows, allowed):
    scores = score_table(queries, key_rows, allowed)
    highest = jnp.max(scores, axis=2, keepdims=True)
    logsum = highest + jnp.log(jnp.sum(jnp.exp(scores - highest), axis=2, keepdims=True))
    weights = jnp.exp(scores - logsum).astype(jnp.bfloat16)
    mixed = jnp.einsum(
        "hqk,khd->qhd", weights, head_view(value_rows), preferred_element_type=jnp.float32
    )
    return (mixed.reshape(queries.shape[0], D).astype(jnp.bfloat16), logsum)


def attention_backward(queries, key_rows, value_rows, allowed, logsum, upstream):
    scale_factor = 1.0 / math.sqrt(HD)
    scores = score_table(queries, key_rows, allowed)
    probs = jnp.exp(scores - logsum)
    rounded = probs.astype(jnp.bfloat16)
    grad_heads = head_view(upstream)
    value_grad = jnp.einsum("hqk,qhd->khd", rounded, grad_heads, preferred_element_type=jnp.float32)
    prob_grad = jnp.einsum(
        "qhd,khd->hqk", grad_heads, head_view(value_rows), preferred_element_type=jnp.float32
    )
    delta_row = jnp.sum(probs * prob_grad, axis=2, keepdims=True)
    score_grad = (probs * (prob_grad - delta_row) * scale_factor).astype(jnp.bfloat16)
    query_grad = jnp.einsum(
        "hqk,khd->qhd", score_grad, head_view(key_rows), preferred_element_type=jnp.float32
    )
    key_grad = jnp.einsum(
        "hqk,qhd->khd", score_grad, head_view(queries), preferred_element_type=jnp.float32
    )
    row_total = queries.shape[0]
    joined = jnp.concatenate(
        [
            query_grad.reshape(row_total, D),
            key_grad.reshape(row_total, D),
            value_grad.reshape(row_total, D),
        ],
        axis=1,
    )
    return joined.astype(jnp.bfloat16)


def adam_update(weights, moments, gradient, rate, decay_rate, unscale):
    scaled_grad = gradient / unscale
    first_moment = beta_one * moments[0] + (1.0 - beta_one) * scaled_grad
    second_moment = beta_two * moments[1] + (1.0 - beta_two) * scaled_grad * scaled_grad
    corrected_first = first_moment / (1.0 - beta_one**STEP)
    corrected_second = second_moment / (1.0 - beta_two**STEP)
    updated = weights - rate * (
        corrected_first / (jnp.sqrt(corrected_second) + adam_eps) + decay_rate * weights
    )
    return (updated, jnp.stack([first_moment, second_moment]))


def column_term(left, right):
    return jnp.einsum("tc,te->ce", left, right, preferred_element_type=jnp.float32)


MESH = pl.DeviceIdType.MESH
WIDE_A = 6 * D
GROUP = 24


def position(n):
    depth = n // 8
    me = lax.axis_index("fsdp")
    return depth, me // 8, (me // 4) % 2, (me // 2) % 2, me % 2


def device_at(z, y, x, c):
    return ((z * 2 + y) * 2 + x) * 2 + c


def greet(partners):
    barrier = pltpu.get_barrier_semaphore()
    for device in partners:
        pl.semaphore_signal(barrier, inc=1, device_id=(device,), device_id_type=MESH)
    pl.semaphore_wait(barrier, len(partners))


def remote(src, dst, send, recv, device):
    return pltpu.make_async_remote_copy(
        src_ref=src,
        dst_ref=dst,
        send_sem=send,
        recv_sem=recv,
        device_id=(device,),
        device_id_type=MESH,
    )


def gather_kernel(n, wide, proj, vec, wide_out, proj_out, vec_out, local, ssem, rsem):
    depth, z, y, x, c = position(n)
    z_peers = [device_at((z + d) % depth, y, x, c) for d in range(1, depth)]
    y_peer, x_peer = device_at(z, 1 - y, x, c), device_at(z, y, 1 - x, c)
    core_peer = device_at(z, y, x, 1 - c)
    greet(z_peers + [y_peer, x_peer, core_peer])
    sends = []
    count = [0]

    def push(src, dst, device, landed):
        k = count[0]
        count[0] = k + 1
        copy = remote(src, dst, ssem.at[k], rsem.at[k], device)
        copy.start()
        sends.append(copy)
        return remote(landed, landed, ssem.at[k], rsem.at[k], device)

    own = [
        pltpu.make_async_copy(wide, wide_out.at[z, y, x, c], local.at[0]),
        pltpu.make_async_copy(proj, proj_out.at[z, y, x, c], local.at[1]),
        pltpu.make_async_copy(vec, vec_out.at[z, y, x, c], local.at[2]),
    ]
    for copy in own:
        copy.start()

    def wide_low(zi, p, q, ci):
        return wide_out.at[zi, p, q, ci, :, pl.ds(0, WIDE_A)]

    def wide_high(zi, p, q, ci):
        return wide_out.at[zi, q, p, ci, :, pl.ds(WIDE_A, wide.shape[1] - WIDE_A)]

    def proj_at(zi, p, q, ci):
        return proj_out.at[zi, q, p, ci]

    def vec_at(zi, p, q, ci):
        return vec_out.at[zi, q, p, ci]

    yx = (y, x, y_peer, x_peer)
    xy = (x, y, x_peer, y_peer)
    streams = [
        (wide.at[:, pl.ds(0, WIDE_A)], wide_low, yx),
        (wide.at[:, pl.ds(WIDE_A, wide.shape[1] - WIDE_A)], wide_high, xy),
        (proj, proj_at, xy),
        (vec, vec_at, xy),
    ]
    every = pl.ds(0, depth)
    from_z = [[] for _ in streams]
    from_first = [[] for _ in streams]
    from_second = [[] for _ in streams]
    from_far = [[] for _ in streams]
    from_core = []
    for d in range(1, depth):
        for s, (mine, at, (p, q, _, _)) in enumerate(streams):
            from_z[s].append(
                push(mine, at(z, p, q, c), z_peers[d - 1], at((z + depth - d) % depth, p, q, c))
            )
    for s, (mine, at, (p, q, first, second)) in enumerate(streams):
        from_first[s].append(push(mine, at(z, p, q, c), first, at(z, 1 - p, q, c)))
        from_second[s].append(push(mine, at(z, p, q, c), second, at(z, p, 1 - q, c)))
    for copy in own:
        copy.wait()
    for d in range(1, depth):
        zi = (z + depth - d) % depth
        for s, (mine, at, (p, q, first, second)) in enumerate(streams):
            from_z[s][d - 1].wait_recv()
            here = at(zi, p, q, c)
            from_first[s].append(push(here, here, first, at(zi, 1 - p, q, c)))
            from_second[s].append(push(here, here, second, at(zi, p, 1 - q, c)))
    for mine, at, (p, q, _, _) in streams:
        here = at(every, p, q, c)
        from_core.append(push(here, here, core_peer, at(every, p, q, 1 - c)))
    for d in range(depth):
        zi = (z + depth - d) % depth
        for s, (mine, at, (p, q, first, second)) in enumerate(streams):
            from_first[s][d].wait_recv()
            here = at(zi, 1 - p, q, c)
            from_far[s].append(push(here, here, second, at(zi, 1 - p, 1 - q, c)))
    for mine, at, (p, q, _, _) in streams:
        here = at(every, 1 - p, q, c)
        from_core.append(push(here, here, core_peer, at(every, 1 - p, q, 1 - c)))
    for s, (mine, at, (p, q, _, _)) in enumerate(streams):
        for d in range(depth):
            from_second[s][d].wait_recv()
        here = at(every, p, 1 - q, c)
        from_core.append(push(here, here, core_peer, at(every, p, 1 - q, 1 - c)))
    for s, (mine, at, (p, q, _, _)) in enumerate(streams):
        for d in range(depth):
            from_far[s][d].wait_recv()
        here = at(every, 1 - p, 1 - q, c)
        from_core.append(push(here, here, core_peer, at(every, 1 - p, 1 - q, 1 - c)))
    for copy in from_core:
        copy.wait_recv()
    for copy in sends:
        copy.wait_send()


def gather_all(n, wide, proj, vec):
    depth = n // 8
    lead = (depth, 2, 2, 2)
    copies = 4 * (depth - 1 + 3 * depth + 4)
    out = tuple(jax.ShapeDtypeStruct(lead + part.shape, part.dtype) for part in (wide, proj, vec))
    space = pl.BlockSpec(memory_space=pl.ANY)
    wide_out, proj_out, vec_out = pl.pallas_call(
        functools.partial(gather_kernel, n),
        out_shape=out,
        in_specs=[space] * 3,
        out_specs=(space,) * 3,
        scratch_shapes=[
            pltpu.SemaphoreType.DMA((3,)),
            pltpu.SemaphoreType.DMA((copies,)),
            pltpu.SemaphoreType.DMA((copies,)),
        ],
        compiler_params=pltpu.CompilerParams(collective_id=0, has_side_effects=True),
    )(wide, proj, vec)
    return (
        wide_out.reshape(n * wide.shape[0], wide.shape[1]),
        proj_out.reshape(n * proj.shape[0], proj.shape[1]),
        vec_out.reshape(n, *vec.shape),
    )


def scatter_kernel(
    n,
    in_a,
    att_a,
    sec_a,
    sec_b,
    hid_b,
    qkv_g,
    res_g,
    pre_g,
    cot,
    vec,
    wide_out,
    proj_out,
    vec_out,
    given,
    kept,
    land_core,
    land_second,
    land_third,
    land_z,
    vec_kept,
    vec_core,
    vec_second,
    vec_third,
    vec_z,
    ssem,
    rsem,
):
    depth, z, y, x, c = position(n)
    z_devices = [device_at((z + d) % depth, y, x, c) for d in range(1, depth)]
    y_peer, x_peer = device_at(z, 1 - y, x, c), device_at(z, y, 1 - x, c)
    core_peer = device_at(z, y, x, 1 - c)
    greet(z_devices + [y_peer, x_peer, core_peer])
    second_peer = (x_peer, y_peer)
    third_peer = (y_peer, x_peer)
    spots = ((x, y), (y, x))
    sends = []
    count = [24]

    def push(src, dst, device):
        k = count[0]
        count[0] = k + 1
        copy = remote(src, dst, ssem.at[k], rsem.at[k], device)
        copy.start()
        sends.append(copy)
        return copy

    vec_copy = push(vec.at[1 - c], vec_core, core_peer)

    def product(left, right):
        return jnp.dot(left, right, preferred_element_type=jnp.float32)

    def block(left, right):
        return product(left, right).reshape(depth, GROUP, D)

    def fill(k, s, half, t, target):
        i = (spots[s][0] + 1 - t // 2) % 2
        j = (spots[s][1] + 1 - t % 2) % 2
        if s == 0:
            left = in_a[half, i, j]
            if k == 0:
                pair = (block(left, qkv_g[:, 0:D]), block(left, qkv_g[:, D : 2 * D]))
            elif k == 1:
                pair = (
                    block(left, qkv_g[:, 2 * D : 3 * D]),
                    block(att_a[half, i, j], res_g[...]),
                )
            else:
                left = sec_a[half, i, j]
                pair = (block(left, pre_g[:, 0:D]), block(left, pre_g[:, D : 2 * D]))
            value = jnp.concatenate(pair, axis=1)
        elif k == 0:
            left = sec_b[half, i, j]
            value = jnp.concatenate(
                (block(left, pre_g[:, 2 * D : 3 * D]), block(left, pre_g[:, 3 * D : 4 * D])), axis=1
            )
        else:
            value = product(hid_b[k - 1, half, i, j], cot[...]).reshape(depth, 2 * GROUP, D)
        target[...] = value.astype(jnp.bfloat16)

    def core_copy(k, s, t):
        q = (k * 2 + s) * 4 + t
        return remote(
            given.at[k, s, t], land_core.at[k, s, t], ssem.at[q], rsem.at[q], core_peer
        )

    def multiply(k):
        def give(t, carry):
            for s in range(2):
                fill(k, s, 1 - c, t, given.at[k, s, t])
                core_copy(k, s, t).start()
            return carry

        def keep(t, carry):
            for s in range(2):
                fill(k, s, c, t, kept.at[k, s, t])
            return carry

        lax.fori_loop(0, 4, give, 0)
        lax.fori_loop(0, 4, keep, 0)

    def merge(target, landed):
        def step(k, carry):
            target[k] = (
                target[k].astype(jnp.float32) + landed[k].astype(jnp.float32)
            ).astype(jnp.bfloat16)
            return carry

        lax.fori_loop(0, depth, step, 0)

    second, third, last = {}, {}, {}

    def stage_second(k):
        for t in range(4):
            for s in range(2):
                core_copy(k, s, t).wait_recv()
                merge(kept.at[k, s, t], land_core.at[k, s, t])
                if t < 2:
                    second[k, s, t] = push(
                        kept.at[k, s, t], land_second.at[k, s, t], second_peer[s]
                    )

    def stage_third(k):
        for t in range(2):
            for s in range(2):
                second[k, s, t].wait_recv()
                merge(kept.at[k, s, 2 + t], land_second.at[k, s, t])
                if t == 0:
                    third[k, s] = push(kept.at[k, s, 2], land_third.at[k, s], third_peer[s])

    def stage_last(k):
        for s in range(2):
            third[k, s].wait_recv()
            merge(kept.at[k, s, 3], land_third.at[k, s])
            last[k, s] = [
                push(kept.at[k, s, 3, (z + d) % depth], land_z.at[k, s, d - 1], z_devices[d - 1])
                for d in range(1, depth)
            ]

    def finish(k):
        for s in range(2):
            total = kept[k, s, 3, z].astype(jnp.float32)
            for d in range(depth - 1):
                last[k, s][d].wait_recv()
                total += land_z[k, s, d].astype(jnp.float32)
            for b in range(2):
                rows = total[b * GROUP : (b + 1) * GROUP]
                if s == 1 and k > 0:
                    first = ((k - 1) * 2 + b) * GROUP
                    proj_out[first : first + GROUP] = rows
                else:
                    column = (6 * s + 2 * k + b) * D
                    wide_out[:, column : column + D] = rows

    multiply(0)
    stage_second(0)
    vec_copy.wait_recv()
    vec_kept[...] = vec[c] + vec_core[...]
    vec_copy = push(vec_kept.at[1 - x], vec_second, x_peer)
    multiply(1)
    stage_second(1)
    stage_third(0)
    vec_copy.wait_recv()
    vec_kept[x] += vec_second[...]
    vec_copy = push(vec_kept.at[x, 1 - y], vec_third, y_peer)
    multiply(2)
    stage_second(2)
    stage_last(0)
    stage_third(1)
    vec_copy.wait_recv()
    vec_kept[x, y] += vec_third[...]
    vec_last = [
        push(vec_kept.at[x, y, (z + d) % depth], vec_z.at[d - 1], z_devices[d - 1])
        for d in range(1, depth)
    ]
    stage_last(1)
    stage_third(2)
    stage_last(2)
    total = vec_kept[x, y, z]
    for d in range(depth - 1):
        vec_last[d].wait_recv()
        total += vec_z[d]
    vec_out[...] = total
    for k in range(3):
        finish(k)
    for k in range(3):
        for s in range(2):
            for t in range(4):
                core_copy(k, s, t).wait_send()
    for copy in sends:
        copy.wait_send()


def by_owner(rows, n, order):
    depth = n // 8
    size = rows.shape[0] // n
    names = {"y": 1, "x": 2, "c": 3}
    split = rows.reshape(depth, 2, 2, 2, size, *rows.shape[1:])
    rest = tuple(range(4, split.ndim))
    return split.transpose(*(names[k] for k in order), 0, *rest)


def scatter_all(n, first_in, attended, second_in, hidden, qkv_grad, resid_half, pre_grad, cot, vec):
    depth = n // 8

    def left(rows, order):
        ordered = by_owner(rows.T, n, order)
        return ordered.reshape(2, 2, 2, -1, rows.shape[0])

    dtype = jnp.bfloat16
    unit = (depth, 2 * GROUP, D)
    tile = vec.shape[1:]
    copies = 24 + 6 * (2 + 1 + depth - 1) + 3 + depth - 1
    space = pl.BlockSpec(memory_space=pltpu.VMEM)
    return pl.pallas_call(
        functools.partial(scatter_kernel, n),
        out_shape=(
            jax.ShapeDtypeStruct((GROUP, 8 * D), jnp.float32),
            jax.ShapeDtypeStruct((4 * GROUP, D), jnp.float32),
            jax.ShapeDtypeStruct(tile, jnp.float32),
        ),
        in_specs=[space] * 10,
        out_specs=(space,) * 3,
        scratch_shapes=[
            pltpu.VMEM((3, 2, 4) + unit, dtype),
            pltpu.VMEM((3, 2, 4) + unit, dtype),
            pltpu.VMEM((3, 2, 4) + unit, dtype),
            pltpu.VMEM((3, 2, 2) + unit, dtype),
            pltpu.VMEM((3, 2) + unit, dtype),
            pltpu.VMEM((3, 2, depth - 1, 2 * GROUP, D), dtype),
            pltpu.VMEM((2, 2, depth) + tile, jnp.float32),
            pltpu.VMEM((2, 2, depth) + tile, jnp.float32),
            pltpu.VMEM((2, depth) + tile, jnp.float32),
            pltpu.VMEM((depth,) + tile, jnp.float32),
            pltpu.VMEM((depth - 1,) + tile, jnp.float32),
            pltpu.SemaphoreType.DMA((copies,)),
            pltpu.SemaphoreType.DMA((copies,)),
        ],
        compiler_params=pltpu.CompilerParams(
            collective_id=1, has_side_effects=True, vmem_limit_bytes=52 * 2**20
        ),
    )(
        left(first_in, "cxy"),
        left(attended, "cxy"),
        left(second_in, "cxy"),
        left(second_in, "cyx"),
        by_owner(hidden.T, n, "cyx")
        .reshape(2, 2, 2, depth, 2, 2 * GROUP, hidden.shape[0])
        .transpose(4, 0, 1, 2, 3, 5, 6)
        .reshape(2, 2, 2, 2, depth * 2 * GROUP, hidden.shape[0]),
        qkv_grad,
        resid_half,
        pre_grad,
        cot,
        by_owner(vec, n, "cxy").reshape(2, 2, 2, depth, *tile),
    )


def to_tile(rows):
    flat = rows.reshape(rows.shape[0], -1)
    return jnp.pad(flat, ((0, 0), (0, 1024 - flat.shape[1]))).reshape(rows.shape[0], 8, 128)


def from_tile(tiles, rows, columns):
    return tiles.reshape(tiles.shape[0], 1024)[:, : rows * columns].reshape(-1, rows, columns)


def body(
    tokens,
    seq_lengths,
    cotangent,
    wide_weights,
    proj_weights,
    vector_params,
    wide_moments,
    proj_moments,
    vector_moments,
):
    shards = (
        wide_weights.astype(jnp.bfloat16),
        proj_weights.astype(jnp.bfloat16),
        vector_params.astype(jnp.bfloat16),
    )
    devices = lax.axis_size("fsdp")
    direct = wide_weights.shape[0] == GROUP and devices % 8 == 0
    vector_rows, vector_columns = vector_params.shape
    if direct:
        wide_full, proj_full, vector_tiles = gather_all(
            devices, shards[0], shards[1], to_tile(shards[2].astype(jnp.float32)[None])[0]
        )
        vector_full = (
            from_tile(vector_tiles, vector_rows, vector_columns)
            .transpose(1, 0, 2)
            .reshape(vector_rows, devices * vector_columns)
        )
    else:
        wide_full, proj_full, vector_full = (
            lax.all_gather(shards[0], "fsdp", axis=0, tiled=True),
            lax.all_gather(shards[1], "fsdp", axis=0, tiled=True),
            lax.all_gather(shards[2], "fsdp", axis=1, tiled=True),
        )
    vectors = vector_full.astype(jnp.float32)
    row_count = tokens.shape[0]
    allowed = allowed_pairs(seq_lengths[0], row_count)
    ratio = FF // D
    local_rows = wide_weights.shape[0]
    unscale = math.sqrt(lax.axis_size("fsdp") * row_count)
    gain_one, shift_one, query_bias, value_bias = (vectors[0], vectors[1], vectors[2], vectors[3])
    out_bias, gain_two, shift_two, proj_bias = (vectors[4], vectors[5], vectors[6], vectors[7])
    fc_bias = vectors[8:].reshape(FF)
    token_float = tokens.astype(jnp.float32)
    first_norm, normed_one, inverse_one = norm_forward(token_float, gain_one, shift_one)
    first_in = first_norm.astype(jnp.bfloat16)
    qkv_bias = jnp.concatenate([query_bias, jnp.zeros_like(query_bias), value_bias])
    qkv_half = (
        jnp.dot(first_in, wide_full[:, : 3 * D], preferred_element_type=jnp.float32) + qkv_bias
    ).astype(jnp.bfloat16)
    queries = qkv_half[:, :D]
    key_rows = qkv_half[:, D : 2 * D]
    value_rows = qkv_half[:, 2 * D :]
    attended, logsum = attention_forward(queries, key_rows, value_rows, allowed)
    residual = (
        token_float
        + jnp.dot(attended, wide_full[:, 3 * D : 4 * D], preferred_element_type=jnp.float32)
        + out_bias
    )
    second_norm, normed_two, inverse_two = norm_forward(residual, gain_two, shift_two)
    second_in = second_norm.astype(jnp.bfloat16)
    before_act = (
        jnp.dot(second_in, wide_full[:, 4 * D :], preferred_element_type=jnp.float32) + fc_bias
    )
    value_part, slope_part = gelu_parts(before_act)
    hidden = value_part.astype(jnp.bfloat16)
    block_output = (
        residual + jnp.dot(hidden, proj_full, preferred_element_type=jnp.float32) + proj_bias
    ).astype(jnp.bfloat16)
    backward_wide, backward_proj, vector_again = wide_full, proj_full, vector_full
    backward_vectors = vector_again.astype(jnp.float32)
    qkv_back = backward_wide[:, : 3 * D]
    out_back = backward_wide[:, 3 * D : 4 * D]
    fc_back = backward_wide[:, 4 * D :]
    cot_float = cotangent.astype(jnp.float32)
    proj_bias_grad = jnp.sum(cot_float, axis=0)
    hidden_grad = jnp.einsum(
        "td,fd->tf", cotangent, backward_proj, preferred_element_type=jnp.float32
    )
    pre_grad = (hidden_grad * slope_part).astype(jnp.bfloat16)
    fc_bias_grad = jnp.sum(pre_grad, axis=0, dtype=jnp.float32)
    second_grad = jnp.einsum("tf,df->td", pre_grad, fc_back, preferred_element_type=jnp.float32)
    resid_norm_grad, gain_two_grad, shift_two_grad = norm_backward(
        second_grad, normed_two, inverse_two, backward_vectors[5]
    )
    resid_grad = cot_float + resid_norm_grad
    mlp_vectors = jnp.concatenate(
        [
            jnp.stack([gain_two_grad, shift_two_grad, proj_bias_grad]),
            fc_bias_grad.reshape(ratio, D),
        ],
        axis=0,
    )
    resid_half = resid_grad.astype(jnp.bfloat16)
    out_bias_grad = jnp.sum(resid_grad, axis=0)
    attended_grad = jnp.einsum(
        "te,de->td", resid_half, out_back, preferred_element_type=jnp.float32
    ).astype(jnp.bfloat16)
    qkv_grad = attention_backward(queries, key_rows, value_rows, allowed, logsum, attended_grad)
    query_bias_grad = jnp.sum(qkv_grad[:, :D], axis=0, dtype=jnp.float32)
    value_bias_grad = jnp.sum(qkv_grad[:, 2 * D :], axis=0, dtype=jnp.float32)
    first_grad = jnp.einsum("tc,dc->td", qkv_grad, qkv_back, preferred_element_type=jnp.float32)
    token_norm_grad, gain_one_grad, shift_one_grad = norm_backward(
        first_grad, normed_one, inverse_one, backward_vectors[0]
    )
    tokens_grad = (resid_grad + token_norm_grad).astype(jnp.bfloat16)
    attn_vectors = jnp.stack(
        [gain_one_grad, shift_one_grad, query_bias_grad, value_bias_grad, out_bias_grad]
    )
    vector_terms = jnp.concatenate([attn_vectors, mlp_vectors], axis=0)
    if direct:
        owned = vector_terms.reshape(vector_rows, devices, vector_columns).transpose(1, 0, 2)
        wide_grad, proj_grad, vector_tile = scatter_all(
            devices,
            first_in,
            attended,
            second_in,
            hidden,
            qkv_grad,
            resid_half,
            pre_grad,
            cotangent,
            to_tile(owned),
        )
        vector_grad = from_tile(vector_tile[None], vector_rows, vector_columns)[0]
    else:
        fc_part = column_term(second_in, pre_grad)
        proj_part = column_term(hidden, cotangent).reshape(
            local_rows * lax.axis_size("fsdp"), ratio * D
        )
        qkv_part = column_term(first_in, qkv_grad)
        out_part = column_term(attended, resid_half)
        joined_shard = lax.psum_scatter(
            jnp.concatenate(
                [
                    jnp.concatenate([qkv_part, out_part], axis=1),
                    jnp.concatenate([fc_part, proj_part], axis=1),
                ],
                axis=1,
            ),
            "fsdp",
            scatter_dimension=0,
            tiled=True,
        )
        wide_grad = joined_shard[:, : 4 * D + FF]
        proj_grad = joined_shard[:, 4 * D + FF :].reshape(local_rows * ratio, D)
        vector_grad = lax.psum_scatter(vector_terms, "fsdp", scatter_dimension=1, tiled=True)
    wide_new, wide_moments_new = adam_update(
        wide_weights, wide_moments, wide_grad, rate_matrix, weight_decay, unscale
    )
    proj_new, proj_moments_new = adam_update(
        proj_weights, proj_moments, proj_grad, rate_matrix, weight_decay, unscale
    )
    vector_new, vector_moments_new = adam_update(
        vector_params, vector_moments, vector_grad, rate_vector, 0.0, unscale
    )
    return (
        block_output,
        tokens_grad,
        wide_grad,
        proj_grad,
        vector_grad,
        wide_new,
        proj_new,
        vector_new,
        wide_moments_new,
        proj_moments_new,
        vector_moments_new,
    )


def solution(mesh):
    placed = (
        P("fsdp", None),
        P("fsdp", None),
        P("fsdp", None),
        P("fsdp", None),
        P("fsdp", None),
        P(None, "fsdp"),
        P(None, "fsdp", None),
        P(None, "fsdp", None),
        P(None, None, "fsdp"),
    )
    return jax.shard_map(
        body,
        mesh=mesh,
        in_specs=placed,
        out_specs=(
            P("fsdp", None),
            P("fsdp", None),
            P("fsdp", None),
            P("fsdp", None),
            P(None, "fsdp"),
            P("fsdp", None),
            P("fsdp", None),
            P(None, "fsdp"),
            P(None, "fsdp", None),
            P(None, "fsdp", None),
            P(None, None, "fsdp"),
        ),
        check_vma=False,
    )
```

```python
import functools
import math

import jax
import jax.numpy as jnp
from jax import lax
from jax.experimental import pallas as pl
from jax.experimental.pallas import tpu as pltpu
from jax.sharding import PartitionSpec as P

D = 768
H = 12
HD = 64
FF = 3072
STEP = 2


norm_eps = 1e-05
beta_one = 0.9
beta_two = 0.95
adam_eps = 1e-08
rate_matrix = 0.02
rate_vector = 0.2
weight_decay = 0.1
gelu_coeff = 0.7978845608028654
masked_score = -1e30


def norm_forward(values, gain_row, offset):
    center = values - jnp.mean(values, axis=1, keepdims=True)
    variance = jnp.mean(center * center, axis=1, keepdims=True)
    inverse = lax.rsqrt(variance + norm_eps)
    normed = center * inverse
    return (normed * gain_row + offset, normed, inverse)


def norm_backward(upstream, normed, inverse, gain_row):
    scaled = upstream * gain_row
    mean_term = jnp.mean(scaled, axis=1, keepdims=True)
    proj_term = jnp.mean(scaled * normed, axis=1, keepdims=True)
    input_grad = inverse * (scaled - mean_term - normed * proj_term)
    return (input_grad, jnp.sum(upstream * normed, axis=0), jnp.sum(upstream, axis=0))


def gelu_parts(before):
    inner_arg = gelu_coeff * (before + 0.044715 * before * before * before)
    tangent = jnp.tanh(inner_arg)
    value_part = 0.5 * before * (1.0 + tangent)
    slope_part = 0.5 * (1.0 + tangent) + 0.5 * before * (1.0 - tangent * tangent) * gelu_coeff * (
        1.0 + 3.0 * 0.044715 * before * before
    )
    return (value_part, slope_part)


def allowed_pairs(length_row, row_count):
    bounds = jnp.cumsum(length_row)
    position = jnp.arange(row_count, dtype=jnp.int32)
    segment = jnp.sum((position[:, None] >= bounds[None, :]).astype(jnp.int32), axis=1)
    return (segment[:, None] == segment[None, :]) & (position[None, :] <= position[:, None])


def head_view(matrix):
    return matrix.reshape(matrix.shape[0], H, HD)


def score_table(queries, key_rows, allowed):
    scale_factor = 1.0 / math.sqrt(HD)
    scores = (
        jnp.einsum(
            "qhd,khd->hqk",
            head_view(queries),
            head_view(key_rows),
            preferred_element_type=jnp.float32,
        )
        * scale_factor
    )
    return jnp.where(allowed[None, :, :], scores, masked_score)


def attention_forward(queries, key_rows, value_rows, allowed):
    scores = score_table(queries, key_rows, allowed)
    highest = jnp.max(scores, axis=2, keepdims=True)
    logsum = highest + jnp.log(jnp.sum(jnp.exp(scores - highest), axis=2, keepdims=True))
    weights = jnp.exp(scores - logsum).astype(jnp.bfloat16)
    mixed = jnp.einsum(
        "hqk,khd->qhd", weights, head_view(value_rows), preferred_element_type=jnp.float32
    )
    return (mixed.reshape(queries.shape[0], D).astype(jnp.bfloat16), logsum)


def attention_backward(queries, key_rows, value_rows, allowed, logsum, upstream):
    scale_factor = 1.0 / math.sqrt(HD)
    scores = score_table(queries, key_rows, allowed)
    probs = jnp.exp(scores - logsum)
    rounded = probs.astype(jnp.bfloat16)
    grad_heads = head_view(upstream)
    value_grad = jnp.einsum("hqk,qhd->khd", rounded, grad_heads, preferred_element_type=jnp.float32)
    prob_grad = jnp.einsum(
        "qhd,khd->hqk", grad_heads, head_view(value_rows), preferred_element_type=jnp.float32
    )
    delta_row = jnp.sum(probs * prob_grad, axis=2, keepdims=True)
    score_grad = (probs * (prob_grad - delta_row) * scale_factor).astype(jnp.bfloat16)
    query_grad = jnp.einsum(
        "hqk,khd->qhd", score_grad, head_view(key_rows), preferred_element_type=jnp.float32
    )
    key_grad = jnp.einsum(
        "hqk,qhd->khd", score_grad, head_view(queries), preferred_element_type=jnp.float32
    )
    row_total = queries.shape[0]
    joined = jnp.concatenate(
        [
            query_grad.reshape(row_total, D),
            key_grad.reshape(row_total, D),
            value_grad.reshape(row_total, D),
        ],
        axis=1,
    )
    return joined.astype(jnp.bfloat16)


def adam_update(weights, moments, gradient, rate, decay_rate, unscale):
    scaled_grad = gradient / unscale
    first_moment = beta_one * moments[0] + (1.0 - beta_one) * scaled_grad
    second_moment = beta_two * moments[1] + (1.0 - beta_two) * scaled_grad * scaled_grad
    corrected_first = first_moment / (1.0 - beta_one**STEP)
    corrected_second = second_moment / (1.0 - beta_two**STEP)
    updated = weights - rate * (
        corrected_first / (jnp.sqrt(corrected_second) + adam_eps) + decay_rate * weights
    )
    return (updated, jnp.stack([first_moment, second_moment]))


def column_term(left, right):
    return jnp.einsum("tc,te->ce", left, right, preferred_element_type=jnp.float32)


MESH = pl.DeviceIdType.MESH
WIDE_A = 6 * D
GROUP = 24


def position(n):
    depth = n // 8
    me = lax.axis_index("fsdp")
    return depth, me // 8, (me // 4) % 2, (me // 2) % 2, me % 2


def device_at(z, y, x, c):
    return ((z * 2 + y) * 2 + x) * 2 + c


def greet(partners):
    barrier = pltpu.get_barrier_semaphore()
    for device in partners:
        pl.semaphore_signal(barrier, inc=1, device_id=(device,), device_id_type=MESH)
    pl.semaphore_wait(barrier, len(partners))


def remote(src, dst, send, recv, device):
    return pltpu.make_async_remote_copy(
        src_ref=src,
        dst_ref=dst,
        send_sem=send,
        recv_sem=recv,
        device_id=(device,),
        device_id_type=MESH,
    )


def gather_kernel(n, wide, proj, vec, wide_out, proj_out, vec_out, local, ssem, rsem):
    depth, z, y, x, c = position(n)
    z_peers = [device_at((z + d) % depth, y, x, c) for d in range(1, depth)]
    y_peer, x_peer = device_at(z, 1 - y, x, c), device_at(z, y, 1 - x, c)
    core_peer = device_at(z, y, x, 1 - c)
    greet(z_peers + [y_peer, x_peer, core_peer])
    sends = []
    count = [0]

    def push(src, dst, device, landed):
        k = count[0]
        count[0] = k + 1
        copy = remote(src, dst, ssem.at[k], rsem.at[k], device)
        copy.start()
        sends.append(copy)
        return remote(landed, landed, ssem.at[k], rsem.at[k], device)

    own = [
        pltpu.make_async_copy(wide, wide_out.at[z, y, x, c], local.at[0]),
        pltpu.make_async_copy(proj, proj_out.at[z, y, x, c], local.at[1]),
        pltpu.make_async_copy(vec, vec_out.at[z, y, x, c], local.at[2]),
    ]
    for copy in own:
        copy.start()

    def wide_low(zi, p, q, ci):
        return wide_out.at[zi, p, q, ci, :, pl.ds(0, WIDE_A)]

    def wide_high(zi, p, q, ci):
        return wide_out.at[zi, q, p, ci, :, pl.ds(WIDE_A, wide.shape[1] - WIDE_A)]

    def proj_at(zi, p, q, ci):
        return proj_out.at[zi, q, p, ci]

    def vec_at(zi, p, q, ci):
        return vec_out.at[zi, q, p, ci]

    yx = (y, x, y_peer, x_peer)
    xy = (x, y, x_peer, y_peer)
    streams = [
        (wide.at[:, pl.ds(0, WIDE_A)], wide_low, yx),
        (wide.at[:, pl.ds(WIDE_A, wide.shape[1] - WIDE_A)], wide_high, xy),
        (proj, proj_at, xy),
        (vec, vec_at, xy),
    ]
    every = pl.ds(0, depth)
    from_z = [[] for _ in streams]
    from_first = [[] for _ in streams]
    from_second = [[] for _ in streams]
    from_far = [[] for _ in streams]
    from_core = []
    for d in range(1, depth):
        for s, (mine, at, (p, q, _, _)) in enumerate(streams):
            from_z[s].append(
                push(mine, at(z, p, q, c), z_peers[d - 1], at((z + depth - d) % depth, p, q, c))
            )
    for s, (mine, at, (p, q, first, second)) in enumerate(streams):
        from_first[s].append(push(mine, at(z, p, q, c), first, at(z, 1 - p, q, c)))
        from_second[s].append(push(mine, at(z, p, q, c), second, at(z, p, 1 - q, c)))
    for copy in own:
        copy.wait()
    for d in range(1, depth):
        zi = (z + depth - d) % depth
        for s, (mine, at, (p, q, first, second)) in enumerate(streams):
            from_z[s][d - 1].wait_recv()
            here = at(zi, p, q, c)
            from_first[s].append(push(here, here, first, at(zi, 1 - p, q, c)))
            from_second[s].append(push(here, here, second, at(zi, p, 1 - q, c)))
    for mine, at, (p, q, _, _) in streams:
        here = at(every, p, q, c)
        from_core.append(push(here, here, core_peer, at(every, p, q, 1 - c)))
    for d in range(depth):
        zi = (z + depth - d) % depth
        for s, (mine, at, (p, q, first, second)) in enumerate(streams):
            from_first[s][d].wait_recv()
            here = at(zi, 1 - p, q, c)
            from_far[s].append(push(here, here, second, at(zi, 1 - p, 1 - q, c)))
    for mine, at, (p, q, _, _) in streams:
        here = at(every, 1 - p, q, c)
        from_core.append(push(here, here, core_peer, at(every, 1 - p, q, 1 - c)))
    for s, (mine, at, (p, q, _, _)) in enumerate(streams):
        for d in range(depth):
            from_second[s][d].wait_recv()
        here = at(every, p, 1 - q, c)
        from_core.append(push(here, here, core_peer, at(every, p, 1 - q, 1 - c)))
    for s, (mine, at, (p, q, _, _)) in enumerate(streams):
        for d in range(depth):
            from_far[s][d].wait_recv()
        here = at(every, 1 - p, 1 - q, c)
        from_core.append(push(here, here, core_peer, at(every, 1 - p, 1 - q, 1 - c)))
    for copy in from_core:
        copy.wait_recv()
    for copy in sends:
        copy.wait_send()


def gather_all(n, wide, proj, vec):
    depth = n // 8
    lead = (depth, 2, 2, 2)
    copies = 4 * (depth - 1 + 3 * depth + 4)
    out = tuple(jax.ShapeDtypeStruct(lead + part.shape, part.dtype) for part in (wide, proj, vec))
    space = pl.BlockSpec(memory_space=pl.ANY)
    wide_out, proj_out, vec_out = pl.pallas_call(
        functools.partial(gather_kernel, n),
        out_shape=out,
        in_specs=[space] * 3,
        out_specs=(space,) * 3,
        scratch_shapes=[
            pltpu.SemaphoreType.DMA((3,)),
            pltpu.SemaphoreType.DMA((copies,)),
            pltpu.SemaphoreType.DMA((copies,)),
        ],
        compiler_params=pltpu.CompilerParams(
            collective_id=0, has_side_effects=True, vmem_limit_bytes=4 * 2**20
        ),
    )(wide, proj, vec)
    return (
        wide_out.reshape(n * wide.shape[0], wide.shape[1]),
        proj_out.reshape(n * proj.shape[0], proj.shape[1]),
        vec_out.reshape(n, *vec.shape),
    )


def scatter_kernel(
    n,
    in_a,
    att_a,
    sec_a,
    sec_b,
    hid_b,
    qkv_g,
    res_g,
    pre_g,
    cot,
    vec,
    wide_out,
    proj_out,
    vec_out,
    given,
    kept,
    land_core,
    land_second,
    land_third,
    land_z,
    vec_kept,
    vec_core,
    vec_second,
    vec_third,
    vec_z,
    ssem,
    rsem,
):
    depth, z, y, x, c = position(n)
    z_devices = [device_at((z + d) % depth, y, x, c) for d in range(1, depth)]
    y_peer, x_peer = device_at(z, 1 - y, x, c), device_at(z, y, 1 - x, c)
    core_peer = device_at(z, y, x, 1 - c)
    greet(z_devices + [y_peer, x_peer, core_peer])
    second_peer = (x_peer, y_peer)
    third_peer = (y_peer, x_peer)
    spots = ((x, y), (y, x))
    sends = []
    count = [24]

    def push(src, dst, device):
        k = count[0]
        count[0] = k + 1
        copy = remote(src, dst, ssem.at[k], rsem.at[k], device)
        copy.start()
        sends.append(copy)
        return copy

    vec_copy = push(vec.at[1 - c], vec_core, core_peer)

    def product(left, right):
        return jnp.dot(left, right, preferred_element_type=jnp.float32)

    def block(left, right):
        return product(left, right).reshape(depth, GROUP, D)

    def fill(k, s, half, t, target):
        i = (spots[s][0] + 1 - t // 2) % 2
        j = (spots[s][1] + 1 - t % 2) % 2
        if s == 0:
            left = in_a[half, i, j]
            if k == 0:
                pair = (block(left, qkv_g[:, 0:D]), block(left, qkv_g[:, D : 2 * D]))
            elif k == 1:
                pair = (
                    block(left, qkv_g[:, 2 * D : 3 * D]),
                    block(att_a[half, i, j], res_g[...]),
                )
            else:
                left = sec_a[half, i, j]
                pair = (block(left, pre_g[:, 0:D]), block(left, pre_g[:, D : 2 * D]))
            value = jnp.concatenate(pair, axis=1)
        elif k == 0:
            left = sec_b[half, i, j]
            value = jnp.concatenate(
                (block(left, pre_g[:, 2 * D : 3 * D]), block(left, pre_g[:, 3 * D : 4 * D])), axis=1
            )
        else:
            value = product(hid_b[k - 1, half, i, j], cot[...]).reshape(depth, 2 * GROUP, D)
        target[...] = value.astype(jnp.bfloat16)

    def core_copy(k, s, t):
        q = (k * 2 + s) * 4 + t
        return remote(
            given.at[k, s, t], land_core.at[k, s, t], ssem.at[q], rsem.at[q], core_peer
        )

    def multiply(k):
        def give(t, carry):
            for s in range(2):
                fill(k, s, 1 - c, t, given.at[k, s, t])
                core_copy(k, s, t).start()
            return carry

        def keep(t, carry):
            for s in range(2):
                fill(k, s, c, t, kept.at[k, s, t])
            return carry

        lax.fori_loop(0, 4, give, 0)
        lax.fori_loop(0, 4, keep, 0)

    def merge(target, landed):
        def step(k, carry):
            target[k] = (
                target[k].astype(jnp.float32) + landed[k].astype(jnp.float32)
            ).astype(jnp.bfloat16)
            return carry

        lax.fori_loop(0, depth, step, 0)

    second, third, last = {}, {}, {}

    def stage_second(k):
        for t in range(4):
            for s in range(2):
                core_copy(k, s, t).wait_recv()
                merge(kept.at[k, s, t], land_core.at[k, s, t])
                if t < 2:
                    second[k, s, t] = push(
                        kept.at[k, s, t], land_second.at[k, s, t], second_peer[s]
                    )

    def stage_third(k):
        for t in range(2):
            for s in range(2):
                second[k, s, t].wait_recv()
                merge(kept.at[k, s, 2 + t], land_second.at[k, s, t])
                if t == 0:
                    third[k, s] = push(kept.at[k, s, 2], land_third.at[k, s], third_peer[s])

    def stage_last(k):
        for s in range(2):
            third[k, s].wait_recv()
            merge(kept.at[k, s, 3], land_third.at[k, s])
            last[k, s] = [
                push(kept.at[k, s, 3, (z + d) % depth], land_z.at[k, s, d - 1], z_devices[d - 1])
                for d in range(1, depth)
            ]

    def finish(k):
        for s in range(2):
            total = kept[k, s, 3, z].astype(jnp.float32)
            for d in range(depth - 1):
                last[k, s][d].wait_recv()
                total += land_z[k, s, d].astype(jnp.float32)
            for b in range(2):
                rows = total[b * GROUP : (b + 1) * GROUP]
                if s == 1 and k > 0:
                    first = ((k - 1) * 2 + b) * GROUP
                    proj_out[first : first + GROUP] = rows
                else:
                    column = (6 * s + 2 * k + b) * D
                    wide_out[:, column : column + D] = rows

    multiply(0)
    stage_second(0)
    vec_copy.wait_recv()
    vec_kept[...] = vec[c] + vec_core[...]
    vec_copy = push(vec_kept.at[1 - x], vec_second, x_peer)
    multiply(1)
    stage_second(1)
    stage_third(0)
    vec_copy.wait_recv()
    vec_kept[x] += vec_second[...]
    vec_copy = push(vec_kept.at[x, 1 - y], vec_third, y_peer)
    multiply(2)
    stage_second(2)
    stage_last(0)
    stage_third(1)
    vec_copy.wait_recv()
    vec_kept[x, y] += vec_third[...]
    vec_last = [
        push(vec_kept.at[x, y, (z + d) % depth], vec_z.at[d - 1], z_devices[d - 1])
        for d in range(1, depth)
    ]
    stage_last(1)
    stage_third(2)
    stage_last(2)
    total = vec_kept[x, y, z]
    for d in range(depth - 1):
        vec_last[d].wait_recv()
        total += vec_z[d]
    vec_out[...] = total
    for k in range(3):
        finish(k)
    for k in range(3):
        for s in range(2):
            for t in range(4):
                core_copy(k, s, t).wait_send()
    for copy in sends:
        copy.wait_send()


def by_owner(rows, n, order):
    depth = n // 8
    size = rows.shape[0] // n
    names = {"y": 1, "x": 2, "c": 3}
    split = rows.reshape(depth, 2, 2, 2, size, *rows.shape[1:])
    rest = tuple(range(4, split.ndim))
    return split.transpose(*(names[k] for k in order), 0, *rest)


def scatter_all(n, first_in, attended, second_in, hidden, qkv_grad, resid_half, pre_grad, cot, vec):
    depth = n // 8

    def left(rows, order):
        ordered = by_owner(rows.T, n, order)
        return ordered.reshape(2, 2, 2, -1, rows.shape[0])

    dtype = jnp.bfloat16
    unit = (depth, 2 * GROUP, D)
    tile = vec.shape[1:]
    copies = 24 + 6 * (2 + 1 + depth - 1) + 3 + depth - 1
    space = pl.BlockSpec(memory_space=pltpu.VMEM)
    return pl.pallas_call(
        functools.partial(scatter_kernel, n),
        out_shape=(
            jax.ShapeDtypeStruct((GROUP, 8 * D), jnp.float32),
            jax.ShapeDtypeStruct((4 * GROUP, D), jnp.float32),
            jax.ShapeDtypeStruct(tile, jnp.float32),
        ),
        in_specs=[space] * 10,
        out_specs=(space,) * 3,
        scratch_shapes=[
            pltpu.VMEM((3, 2, 4) + unit, dtype),
            pltpu.VMEM((3, 2, 4) + unit, dtype),
            pltpu.VMEM((3, 2, 4) + unit, dtype),
            pltpu.VMEM((3, 2, 2) + unit, dtype),
            pltpu.VMEM((3, 2) + unit, dtype),
            pltpu.VMEM((3, 2, depth - 1, 2 * GROUP, D), dtype),
            pltpu.VMEM((2, 2, depth) + tile, jnp.float32),
            pltpu.VMEM((2, 2, depth) + tile, jnp.float32),
            pltpu.VMEM((2, depth) + tile, jnp.float32),
            pltpu.VMEM((depth,) + tile, jnp.float32),
            pltpu.VMEM((depth - 1,) + tile, jnp.float32),
            pltpu.SemaphoreType.DMA((copies,)),
            pltpu.SemaphoreType.DMA((copies,)),
        ],
        compiler_params=pltpu.CompilerParams(
            collective_id=1, has_side_effects=True, vmem_limit_bytes=40 * 2**20
        ),
    )(
        left(first_in, "cxy"),
        left(attended, "cxy"),
        left(second_in, "cxy"),
        left(second_in, "cyx"),
        by_owner(hidden.T, n, "cyx")
        .reshape(2, 2, 2, depth, 2, 2 * GROUP, hidden.shape[0])
        .transpose(4, 0, 1, 2, 3, 5, 6)
        .reshape(2, 2, 2, 2, depth * 2 * GROUP, hidden.shape[0]),
        qkv_grad,
        resid_half,
        pre_grad,
        cot,
        by_owner(vec, n, "cxy").reshape(2, 2, 2, depth, *tile),
    )


def to_tile(rows):
    flat = rows.reshape(rows.shape[0], -1)
    return jnp.pad(flat, ((0, 0), (0, 1024 - flat.shape[1]))).reshape(rows.shape[0], 8, 128)


def from_tile(tiles, rows, columns):
    return tiles.reshape(tiles.shape[0], 1024)[:, : rows * columns].reshape(-1, rows, columns)


def body(
    tokens,
    seq_lengths,
    cotangent,
    wide_weights,
    proj_weights,
    vector_params,
    wide_moments,
    proj_moments,
    vector_moments,
):
    shards = (
        wide_weights.astype(jnp.bfloat16),
        proj_weights.astype(jnp.bfloat16),
        vector_params.astype(jnp.bfloat16),
    )
    devices = lax.axis_size("fsdp")
    direct = wide_weights.shape[0] == GROUP and devices % 8 == 0
    vector_rows, vector_columns = vector_params.shape
    if direct:
        wide_full, proj_full, vector_tiles = gather_all(
            devices, shards[0], shards[1], to_tile(shards[2].astype(jnp.float32)[None])[0]
        )
        vector_full = (
            from_tile(vector_tiles, vector_rows, vector_columns)
            .transpose(1, 0, 2)
            .reshape(vector_rows, devices * vector_columns)
        )
    else:
        wide_full, proj_full, vector_full = (
            lax.all_gather(shards[0], "fsdp", axis=0, tiled=True),
            lax.all_gather(shards[1], "fsdp", axis=0, tiled=True),
            lax.all_gather(shards[2], "fsdp", axis=1, tiled=True),
        )
    vectors = vector_full.astype(jnp.float32)
    row_count = tokens.shape[0]
    allowed = allowed_pairs(seq_lengths[0], row_count)
    ratio = FF // D
    local_rows = wide_weights.shape[0]
    unscale = math.sqrt(lax.axis_size("fsdp") * row_count)
    gain_one, shift_one, query_bias, value_bias = (vectors[0], vectors[1], vectors[2], vectors[3])
    out_bias, gain_two, shift_two, proj_bias = (vectors[4], vectors[5], vectors[6], vectors[7])
    fc_bias = vectors[8:].reshape(FF)
    token_float = tokens.astype(jnp.float32)
    first_norm, normed_one, inverse_one = norm_forward(token_float, gain_one, shift_one)
    first_in = first_norm.astype(jnp.bfloat16)
    qkv_bias = jnp.concatenate([query_bias, jnp.zeros_like(query_bias), value_bias])
    qkv_half = (
        jnp.dot(first_in, wide_full[:, : 3 * D], preferred_element_type=jnp.float32) + qkv_bias
    ).astype(jnp.bfloat16)
    queries = qkv_half[:, :D]
    key_rows = qkv_half[:, D : 2 * D]
    value_rows = qkv_half[:, 2 * D :]
    attended, logsum = attention_forward(queries, key_rows, value_rows, allowed)
    residual = (
        token_float
        + jnp.dot(attended, wide_full[:, 3 * D : 4 * D], preferred_element_type=jnp.float32)
        + out_bias
    )
    second_norm, normed_two, inverse_two = norm_forward(residual, gain_two, shift_two)
    second_in = second_norm.astype(jnp.bfloat16)
    before_act = (
        jnp.dot(second_in, wide_full[:, 4 * D :], preferred_element_type=jnp.float32) + fc_bias
    )
    value_part, slope_part = gelu_parts(before_act)
    hidden = value_part.astype(jnp.bfloat16)
    block_output = (
        residual + jnp.dot(hidden, proj_full, preferred_element_type=jnp.float32) + proj_bias
    ).astype(jnp.bfloat16)
    backward_wide, backward_proj, vector_again = wide_full, proj_full, vector_full
    backward_vectors = vector_again.astype(jnp.float32)
    qkv_back = backward_wide[:, : 3 * D]
    out_back = backward_wide[:, 3 * D : 4 * D]
    fc_back = backward_wide[:, 4 * D :]
    cot_float = cotangent.astype(jnp.float32)
    proj_bias_grad = jnp.sum(cot_float, axis=0)
    hidden_grad = jnp.einsum(
        "td,fd->tf", cotangent, backward_proj, preferred_element_type=jnp.float32
    )
    pre_grad = (hidden_grad * slope_part).astype(jnp.bfloat16)
    fc_bias_grad = jnp.sum(pre_grad, axis=0, dtype=jnp.float32)
    second_grad = jnp.einsum("tf,df->td", pre_grad, fc_back, preferred_element_type=jnp.float32)
    resid_norm_grad, gain_two_grad, shift_two_grad = norm_backward(
        second_grad, normed_two, inverse_two, backward_vectors[5]
    )
    resid_grad = cot_float + resid_norm_grad
    mlp_vectors = jnp.concatenate(
        [
            jnp.stack([gain_two_grad, shift_two_grad, proj_bias_grad]),
            fc_bias_grad.reshape(ratio, D),
        ],
        axis=0,
    )
    resid_half = resid_grad.astype(jnp.bfloat16)
    out_bias_grad = jnp.sum(resid_grad, axis=0)
    attended_grad = jnp.einsum(
        "te,de->td", resid_half, out_back, preferred_element_type=jnp.float32
    ).astype(jnp.bfloat16)
    qkv_grad = attention_backward(queries, key_rows, value_rows, allowed, logsum, attended_grad)
    query_bias_grad = jnp.sum(qkv_grad[:, :D], axis=0, dtype=jnp.float32)
    value_bias_grad = jnp.sum(qkv_grad[:, 2 * D :], axis=0, dtype=jnp.float32)
    first_grad = jnp.einsum("tc,dc->td", qkv_grad, qkv_back, preferred_element_type=jnp.float32)
    token_norm_grad, gain_one_grad, shift_one_grad = norm_backward(
        first_grad, normed_one, inverse_one, backward_vectors[0]
    )
    tokens_grad = (resid_grad + token_norm_grad).astype(jnp.bfloat16)
    attn_vectors = jnp.stack(
        [gain_one_grad, shift_one_grad, query_bias_grad, value_bias_grad, out_bias_grad]
    )
    vector_terms = jnp.concatenate([attn_vectors, mlp_vectors], axis=0)
    if direct:
        owned = vector_terms.reshape(vector_rows, devices, vector_columns).transpose(1, 0, 2)
        wide_grad, proj_grad, vector_tile = scatter_all(
            devices,
            first_in,
            attended,
            second_in,
            hidden,
            qkv_grad,
            resid_half,
            pre_grad,
            cotangent,
            to_tile(owned),
        )
        vector_grad = from_tile(vector_tile[None], vector_rows, vector_columns)[0]
    else:
        fc_part = column_term(second_in, pre_grad)
        proj_part = column_term(hidden, cotangent).reshape(
            local_rows * lax.axis_size("fsdp"), ratio * D
        )
        qkv_part = column_term(first_in, qkv_grad)
        out_part = column_term(attended, resid_half)
        joined_shard = lax.psum_scatter(
            jnp.concatenate(
                [
                    jnp.concatenate([qkv_part, out_part], axis=1),
                    jnp.concatenate([fc_part, proj_part], axis=1),
                ],
                axis=1,
            ),
            "fsdp",
            scatter_dimension=0,
            tiled=True,
        )
        wide_grad = joined_shard[:, : 4 * D + FF]
        proj_grad = joined_shard[:, 4 * D + FF :].reshape(local_rows * ratio, D)
        vector_grad = lax.psum_scatter(vector_terms, "fsdp", scatter_dimension=1, tiled=True)
    wide_new, wide_moments_new = adam_update(
        wide_weights, wide_moments, wide_grad, rate_matrix, weight_decay, unscale
    )
    proj_new, proj_moments_new = adam_update(
        proj_weights, proj_moments, proj_grad, rate_matrix, weight_decay, unscale
    )
    vector_new, vector_moments_new = adam_update(
        vector_params, vector_moments, vector_grad, rate_vector, 0.0, unscale
    )
    return (
        block_output,
        tokens_grad,
        wide_grad,
        proj_grad,
        vector_grad,
        wide_new,
        proj_new,
        vector_new,
        wide_moments_new,
        proj_moments_new,
        vector_moments_new,
    )


def solution(mesh):
    placed = (
        P("fsdp", None),
        P("fsdp", None),
        P("fsdp", None),
        P("fsdp", None),
        P("fsdp", None),
        P(None, "fsdp"),
        P(None, "fsdp", None),
        P(None, "fsdp", None),
        P(None, None, "fsdp"),
    )
    return jax.shard_map(
        body,
        mesh=mesh,
        in_specs=placed,
        out_specs=(
            P("fsdp", None),
            P("fsdp", None),
            P("fsdp", None),
            P("fsdp", None),
            P(None, "fsdp"),
            P("fsdp", None),
            P("fsdp", None),
            P(None, "fsdp"),
            P(None, "fsdp", None),
            P(None, "fsdp", None),
            P(None, None, "fsdp"),
        ),
        check_vma=False,
    )
```

```python
import functools
import math

import jax
import jax.numpy as jnp
from jax import lax
from jax.experimental import pallas as pl
from jax.experimental.pallas import tpu as pltpu
from jax.sharding import PartitionSpec as P

D = 768
H = 12
HD = 64
FF = 3072
STEP = 2


norm_eps = 1e-05
beta_one = 0.9
beta_two = 0.95
adam_eps = 1e-08
rate_matrix = 0.02
rate_vector = 0.2
weight_decay = 0.1
gelu_coeff = 0.7978845608028654
masked_score = -1e30


def norm_forward(values, gain_row, offset):
    center = values - jnp.mean(values, axis=1, keepdims=True)
    variance = jnp.mean(center * center, axis=1, keepdims=True)
    inverse = lax.rsqrt(variance + norm_eps)
    normed = center * inverse
    return (normed * gain_row + offset, normed, inverse)


def norm_backward(upstream, normed, inverse, gain_row):
    scaled = upstream * gain_row
    mean_term = jnp.mean(scaled, axis=1, keepdims=True)
    proj_term = jnp.mean(scaled * normed, axis=1, keepdims=True)
    input_grad = inverse * (scaled - mean_term - normed * proj_term)
    return (input_grad, jnp.sum(upstream * normed, axis=0), jnp.sum(upstream, axis=0))


def gelu_parts(before):
    inner_arg = gelu_coeff * (before + 0.044715 * before * before * before)
    tangent = jnp.tanh(inner_arg)
    value_part = 0.5 * before * (1.0 + tangent)
    slope_part = 0.5 * (1.0 + tangent) + 0.5 * before * (1.0 - tangent * tangent) * gelu_coeff * (
        1.0 + 3.0 * 0.044715 * before * before
    )
    return (value_part, slope_part)


def allowed_pairs(length_row, row_count):
    bounds = jnp.cumsum(length_row)
    position = jnp.arange(row_count, dtype=jnp.int32)
    segment = jnp.sum((position[:, None] >= bounds[None, :]).astype(jnp.int32), axis=1)
    return (segment[:, None] == segment[None, :]) & (position[None, :] <= position[:, None])


def head_view(matrix):
    return matrix.reshape(matrix.shape[0], H, HD)


def score_table(queries, key_rows, allowed):
    scale_factor = 1.0 / math.sqrt(HD)
    scores = (
        jnp.einsum(
            "qhd,khd->hqk",
            head_view(queries),
            head_view(key_rows),
            preferred_element_type=jnp.float32,
        )
        * scale_factor
    )
    return jnp.where(allowed[None, :, :], scores, masked_score)


def attention_forward(queries, key_rows, value_rows, allowed):
    scores = score_table(queries, key_rows, allowed)
    highest = jnp.max(scores, axis=2, keepdims=True)
    logsum = highest + jnp.log(jnp.sum(jnp.exp(scores - highest), axis=2, keepdims=True))
    weights = jnp.exp(scores - logsum).astype(jnp.bfloat16)
    mixed = jnp.einsum(
        "hqk,khd->qhd", weights, head_view(value_rows), preferred_element_type=jnp.float32
    )
    return (mixed.reshape(queries.shape[0], D).astype(jnp.bfloat16), logsum)


def attention_backward(queries, key_rows, value_rows, allowed, logsum, upstream):
    scale_factor = 1.0 / math.sqrt(HD)
    scores = score_table(queries, key_rows, allowed)
    probs = jnp.exp(scores - logsum)
    rounded = probs.astype(jnp.bfloat16)
    grad_heads = head_view(upstream)
    value_grad = jnp.einsum("hqk,qhd->khd", rounded, grad_heads, preferred_element_type=jnp.float32)
    prob_grad = jnp.einsum(
        "qhd,khd->hqk", grad_heads, head_view(value_rows), preferred_element_type=jnp.float32
    )
    delta_row = jnp.sum(probs * prob_grad, axis=2, keepdims=True)
    score_grad = (probs * (prob_grad - delta_row) * scale_factor).astype(jnp.bfloat16)
    query_grad = jnp.einsum(
        "hqk,khd->qhd", score_grad, head_view(key_rows), preferred_element_type=jnp.float32
    )
    key_grad = jnp.einsum(
        "hqk,qhd->khd", score_grad, head_view(queries), preferred_element_type=jnp.float32
    )
    row_total = queries.shape[0]
    joined = jnp.concatenate(
        [
            query_grad.reshape(row_total, D),
            key_grad.reshape(row_total, D),
            value_grad.reshape(row_total, D),
        ],
        axis=1,
    )
    return joined.astype(jnp.bfloat16)


def adam_update(weights, moments, gradient, rate, decay_rate, unscale):
    scaled_grad = gradient / unscale
    first_moment = beta_one * moments[0] + (1.0 - beta_one) * scaled_grad
    second_moment = beta_two * moments[1] + (1.0 - beta_two) * scaled_grad * scaled_grad
    corrected_first = first_moment / (1.0 - beta_one**STEP)
    corrected_second = second_moment / (1.0 - beta_two**STEP)
    updated = weights - rate * (
        corrected_first / (jnp.sqrt(corrected_second) + adam_eps) + decay_rate * weights
    )
    return (updated, jnp.stack([first_moment, second_moment]))


def column_term(left, right):
    return jnp.einsum("tc,te->ce", left, right, preferred_element_type=jnp.float32)


MESH = pl.DeviceIdType.MESH
WIDE_A = 6 * D
GROUP = 24


def position(n):
    depth = n // 8
    me = lax.axis_index("fsdp")
    return depth, me // 8, (me // 4) % 2, (me // 2) % 2, me % 2


def device_at(z, y, x, c):
    return ((z * 2 + y) * 2 + x) * 2 + c


def greet(partners):
    barrier = pltpu.get_barrier_semaphore()
    for device in partners:
        pl.semaphore_signal(barrier, inc=1, device_id=(device,), device_id_type=MESH)
    pl.semaphore_wait(barrier, len(partners))


def remote(src, dst, send, recv, device):
    return pltpu.make_async_remote_copy(
        src_ref=src,
        dst_ref=dst,
        send_sem=send,
        recv_sem=recv,
        device_id=(device,),
        device_id_type=MESH,
    )


def gather_kernel(n, wide, proj, vec, wide_out, proj_out, vec_out, local, ssem, rsem):
    depth, z, y, x, c = position(n)
    z_peers = [device_at((z + d) % depth, y, x, c) for d in range(1, depth)]
    y_peer, x_peer = device_at(z, 1 - y, x, c), device_at(z, y, 1 - x, c)
    core_peer = device_at(z, y, x, 1 - c)
    greet(z_peers + [y_peer, x_peer, core_peer])
    sends = []
    count = [0]

    def push(src, dst, device, landed):
        k = count[0]
        count[0] = k + 1
        copy = remote(src, dst, ssem.at[k], rsem.at[k], device)
        copy.start()
        sends.append(copy)
        return remote(landed, landed, ssem.at[k], rsem.at[k], device)

    own = [
        pltpu.make_async_copy(wide, wide_out.at[z, y, x, c], local.at[0]),
        pltpu.make_async_copy(proj, proj_out.at[z, y, x, c], local.at[1]),
        pltpu.make_async_copy(vec, vec_out.at[z, y, x, c], local.at[2]),
    ]
    for copy in own:
        copy.start()

    def wide_low(zi, p, q, ci):
        return wide_out.at[zi, p, q, ci, :, pl.ds(0, WIDE_A)]

    def wide_high(zi, p, q, ci):
        return wide_out.at[zi, q, p, ci, :, pl.ds(WIDE_A, wide.shape[1] - WIDE_A)]

    def proj_at(zi, p, q, ci):
        return proj_out.at[zi, q, p, ci]

    def vec_at(zi, p, q, ci):
        return vec_out.at[zi, q, p, ci]

    yx = (y, x, y_peer, x_peer)
    xy = (x, y, x_peer, y_peer)
    streams = [
        (wide.at[:, pl.ds(0, WIDE_A)], wide_low, yx),
        (wide.at[:, pl.ds(WIDE_A, wide.shape[1] - WIDE_A)], wide_high, xy),
        (proj, proj_at, xy),
        (vec, vec_at, xy),
    ]
    every = pl.ds(0, depth)
    from_z = [[] for _ in streams]
    from_first = [[] for _ in streams]
    from_second = [[] for _ in streams]
    from_far = [[] for _ in streams]
    from_core = []
    for d in range(1, depth):
        for s, (mine, at, (p, q, _, _)) in enumerate(streams):
            from_z[s].append(
                push(mine, at(z, p, q, c), z_peers[d - 1], at((z + depth - d) % depth, p, q, c))
            )
    for s, (mine, at, (p, q, first, second)) in enumerate(streams):
        from_first[s].append(push(mine, at(z, p, q, c), first, at(z, 1 - p, q, c)))
        from_second[s].append(push(mine, at(z, p, q, c), second, at(z, p, 1 - q, c)))
    for copy in own:
        copy.wait()
    for d in range(1, depth):
        zi = (z + depth - d) % depth
        for s, (mine, at, (p, q, first, second)) in enumerate(streams):
            from_z[s][d - 1].wait_recv()
            here = at(zi, p, q, c)
            from_first[s].append(push(here, here, first, at(zi, 1 - p, q, c)))
            from_second[s].append(push(here, here, second, at(zi, p, 1 - q, c)))
    for mine, at, (p, q, _, _) in streams:
        here = at(every, p, q, c)
        from_core.append(push(here, here, core_peer, at(every, p, q, 1 - c)))
    for d in range(depth):
        zi = (z + depth - d) % depth
        for s, (mine, at, (p, q, first, second)) in enumerate(streams):
            from_first[s][d].wait_recv()
            here = at(zi, 1 - p, q, c)
            from_far[s].append(push(here, here, second, at(zi, 1 - p, 1 - q, c)))
    for mine, at, (p, q, _, _) in streams:
        here = at(every, 1 - p, q, c)
        from_core.append(push(here, here, core_peer, at(every, 1 - p, q, 1 - c)))
    for s, (mine, at, (p, q, _, _)) in enumerate(streams):
        for d in range(depth):
            from_second[s][d].wait_recv()
        here = at(every, p, 1 - q, c)
        from_core.append(push(here, here, core_peer, at(every, p, 1 - q, 1 - c)))
    for s, (mine, at, (p, q, _, _)) in enumerate(streams):
        for d in range(depth):
            from_far[s][d].wait_recv()
        here = at(every, 1 - p, 1 - q, c)
        from_core.append(push(here, here, core_peer, at(every, 1 - p, 1 - q, 1 - c)))
    for copy in from_core:
        copy.wait_recv()
    for copy in sends:
        copy.wait_send()


def gather_all(n, wide, proj, vec):
    depth = n // 8
    lead = (depth, 2, 2, 2)
    copies = 4 * (depth - 1 + 3 * depth + 4)
    out = tuple(jax.ShapeDtypeStruct(lead + part.shape, part.dtype) for part in (wide, proj, vec))
    space = pl.BlockSpec(memory_space=pl.ANY)
    wide_out, proj_out, vec_out = pl.pallas_call(
        functools.partial(gather_kernel, n),
        out_shape=out,
        in_specs=[space] * 3,
        out_specs=(space,) * 3,
        scratch_shapes=[
            pltpu.SemaphoreType.DMA((3,)),
            pltpu.SemaphoreType.DMA((copies,)),
            pltpu.SemaphoreType.DMA((copies,)),
        ],
        compiler_params=pltpu.CompilerParams(collective_id=0, has_side_effects=True),
    )(wide, proj, vec)
    return (
        wide_out.reshape(n * wide.shape[0], wide.shape[1]),
        proj_out.reshape(n * proj.shape[0], proj.shape[1]),
        vec_out.reshape(n, *vec.shape),
    )


def scatter_kernel(
    n,
    in_a,
    att_a,
    sec_a,
    sec_b,
    hid_b,
    qkv_g,
    res_g,
    pre_g,
    cot,
    vec,
    wide_out,
    proj_out,
    vec_out,
    given,
    kept,
    land_core,
    land_second,
    land_third,
    land_z,
    vec_kept,
    vec_core,
    vec_second,
    vec_third,
    vec_z,
    ssem,
    rsem,
):
    depth, z, y, x, c = position(n)
    z_devices = [device_at((z + d) % depth, y, x, c) for d in range(1, depth)]
    y_peer, x_peer = device_at(z, 1 - y, x, c), device_at(z, y, 1 - x, c)
    core_peer = device_at(z, y, x, 1 - c)
    greet(z_devices + [y_peer, x_peer, core_peer])
    second_peer = (x_peer, y_peer)
    third_peer = (y_peer, x_peer)
    spots = ((x, y), (y, x))
    sends = []
    count = [24]

    def push(src, dst, device):
        k = count[0]
        count[0] = k + 1
        copy = remote(src, dst, ssem.at[k], rsem.at[k], device)
        copy.start()
        sends.append(copy)
        return copy

    vec_copy = push(vec.at[1 - c], vec_core, core_peer)

    def product(left, right):
        return jnp.dot(left, right, preferred_element_type=jnp.float32)

    def block(left, right):
        return product(left, right).reshape(depth, GROUP, D)

    def fill(k, s, half, t, target):
        i = (spots[s][0] + 1 - t // 2) % 2
        j = (spots[s][1] + 1 - t % 2) % 2
        if s == 0:
            left = in_a[half, i, j]
            if k == 0:
                pair = (block(left, qkv_g[:, 0:D]), block(left, qkv_g[:, D : 2 * D]))
            elif k == 1:
                pair = (
                    block(left, qkv_g[:, 2 * D : 3 * D]),
                    block(att_a[half, i, j], res_g[...]),
                )
            else:
                left = sec_a[half, i, j]
                pair = (block(left, pre_g[:, 0:D]), block(left, pre_g[:, D : 2 * D]))
            value = jnp.concatenate(pair, axis=1)
        elif k == 0:
            left = sec_b[half, i, j]
            value = jnp.concatenate(
                (block(left, pre_g[:, 2 * D : 3 * D]), block(left, pre_g[:, 3 * D : 4 * D])), axis=1
            )
        else:
            value = product(hid_b[k - 1, half, i, j], cot[...]).reshape(depth, 2 * GROUP, D)
        target[...] = value.astype(jnp.bfloat16)

    def core_copy(k, s, t):
        q = (k * 2 + s) * 4 + t
        return remote(
            given.at[k, s, t], land_core.at[k, s, t], ssem.at[q], rsem.at[q], core_peer
        )

    def multiply(k):
        def give(t, carry):
            for s in range(2):
                fill(k, s, 1 - c, t, given.at[k, s, t])
                core_copy(k, s, t).start()
            return carry

        def keep(t, carry):
            for s in range(2):
                fill(k, s, c, t, kept.at[k, s, t])
            return carry

        lax.fori_loop(0, 4, give, 0)
        lax.fori_loop(0, 4, keep, 0)

    def merge(target, landed):
        def step(k, carry):
            target[k] = (
                target[k].astype(jnp.float32) + landed[k].astype(jnp.float32)
            ).astype(jnp.bfloat16)
            return carry

        lax.fori_loop(0, depth, step, 0)

    second, third, last = {}, {}, {}

    def stage_second(k):
        for t in range(4):
            for s in range(2):
                core_copy(k, s, t).wait_recv()
                merge(kept.at[k, s, t], land_core.at[k, s, t])
                if t < 2:
                    second[k, s, t] = push(
                        kept.at[k, s, t], land_second.at[k, s, t], second_peer[s]
                    )

    def stage_third(k):
        for t in range(2):
            for s in range(2):
                second[k, s, t].wait_recv()
                merge(kept.at[k, s, 2 + t], land_second.at[k, s, t])
                if t == 0:
                    third[k, s] = push(kept.at[k, s, 2], land_third.at[k, s], third_peer[s])

    def stage_last(k):
        for s in range(2):
            third[k, s].wait_recv()
            merge(kept.at[k, s, 3], land_third.at[k, s])
            last[k, s] = [
                push(kept.at[k, s, 3, (z + d) % depth], land_z.at[k, s, d - 1], z_devices[d - 1])
                for d in range(1, depth)
            ]

    def finish(k):
        for s in range(2):
            total = kept[k, s, 3, z].astype(jnp.float32)
            for d in range(depth - 1):
                last[k, s][d].wait_recv()
                total += land_z[k, s, d].astype(jnp.float32)
            for b in range(2):
                rows = total[b * GROUP : (b + 1) * GROUP]
                if s == 1 and k > 0:
                    first = ((k - 1) * 2 + b) * GROUP
                    proj_out[first : first + GROUP] = rows
                else:
                    column = (6 * s + 2 * k + b) * D
                    wide_out[:, column : column + D] = rows

    multiply(0)
    stage_second(0)
    vec_copy.wait_recv()
    vec_kept[...] = vec[c] + vec_core[...]
    vec_copy = push(vec_kept.at[1 - x], vec_second, x_peer)
    multiply(1)
    stage_second(1)
    stage_third(0)
    vec_copy.wait_recv()
    vec_kept[x] += vec_second[...]
    vec_copy = push(vec_kept.at[x, 1 - y], vec_third, y_peer)
    multiply(2)
    stage_second(2)
    stage_last(0)
    stage_third(1)
    vec_copy.wait_recv()
    vec_kept[x, y] += vec_third[...]
    vec_last = [
        push(vec_kept.at[x, y, (z + d) % depth], vec_z.at[d - 1], z_devices[d - 1])
        for d in range(1, depth)
    ]
    stage_last(1)
    stage_third(2)
    finish(0)
    stage_last(2)
    total = vec_kept[x, y, z]
    for d in range(depth - 1):
        vec_last[d].wait_recv()
        total += vec_z[d]
    vec_out[...] = total
    finish(1)
    finish(2)
    for k in range(3):
        for s in range(2):
            for t in range(4):
                core_copy(k, s, t).wait_send()
    for copy in sends:
        copy.wait_send()


def by_owner(rows, n, order):
    depth = n // 8
    size = rows.shape[0] // n
    names = {"y": 1, "x": 2, "c": 3}
    split = rows.reshape(depth, 2, 2, 2, size, *rows.shape[1:])
    rest = tuple(range(4, split.ndim))
    return split.transpose(*(names[k] for k in order), 0, *rest)


def scatter_all(n, first_in, attended, second_in, hidden, qkv_grad, resid_half, pre_grad, cot, vec):
    depth = n // 8

    def left(rows, order):
        ordered = by_owner(rows.T, n, order)
        return ordered.reshape(2, 2, 2, -1, rows.shape[0])

    dtype = jnp.bfloat16
    unit = (depth, 2 * GROUP, D)
    tile = vec.shape[1:]
    copies = 24 + 6 * (2 + 1 + depth - 1) + 3 + depth - 1
    space = pl.BlockSpec(memory_space=pltpu.VMEM)
    return pl.pallas_call(
        functools.partial(scatter_kernel, n),
        out_shape=(
            jax.ShapeDtypeStruct((GROUP, 8 * D), jnp.float32),
            jax.ShapeDtypeStruct((4 * GROUP, D), jnp.float32),
            jax.ShapeDtypeStruct(tile, jnp.float32),
        ),
        in_specs=[space] * 10,
        out_specs=(space,) * 3,
        scratch_shapes=[
            pltpu.VMEM((3, 2, 4) + unit, dtype),
            pltpu.VMEM((3, 2, 4) + unit, dtype),
            pltpu.VMEM((3, 2, 4) + unit, dtype),
            pltpu.VMEM((3, 2, 2) + unit, dtype),
            pltpu.VMEM((3, 2) + unit, dtype),
            pltpu.VMEM((3, 2, depth - 1, 2 * GROUP, D), dtype),
            pltpu.VMEM((2, 2, depth) + tile, jnp.float32),
            pltpu.VMEM((2, 2, depth) + tile, jnp.float32),
            pltpu.VMEM((2, depth) + tile, jnp.float32),
            pltpu.VMEM((depth,) + tile, jnp.float32),
            pltpu.VMEM((depth - 1,) + tile, jnp.float32),
            pltpu.SemaphoreType.DMA((copies,)),
            pltpu.SemaphoreType.DMA((copies,)),
        ],
        compiler_params=pltpu.CompilerParams(
            collective_id=1, has_side_effects=True, vmem_limit_bytes=52 * 2**20
        ),
    )(
        left(first_in, "cxy"),
        left(attended, "cxy"),
        left(second_in, "cxy"),
        left(second_in, "cyx"),
        by_owner(hidden.T, n, "cyx")
        .reshape(2, 2, 2, depth, 2, 2 * GROUP, hidden.shape[0])
        .transpose(4, 0, 1, 2, 3, 5, 6)
        .reshape(2, 2, 2, 2, depth * 2 * GROUP, hidden.shape[0]),
        qkv_grad,
        resid_half,
        pre_grad,
        cot,
        by_owner(vec, n, "cxy").reshape(2, 2, 2, depth, *tile),
    )


def to_tile(rows):
    flat = rows.reshape(rows.shape[0], -1)
    return jnp.pad(flat, ((0, 0), (0, 1024 - flat.shape[1]))).reshape(rows.shape[0], 8, 128)


def from_tile(tiles, rows, columns):
    return tiles.reshape(tiles.shape[0], 1024)[:, : rows * columns].reshape(-1, rows, columns)


MLP_TILE = 512


def mlp_kernel(second_in, cot, wide, proj, bias, hidden_out, pre_out, mixed, second_grad, bias_out):
    @pl.when(pl.program_id(0) == 0)
    def _():
        mixed[...] = jnp.zeros_like(mixed)
        second_grad[...] = jnp.zeros_like(second_grad)

    before = (
        jnp.dot(second_in[...], wide[...], preferred_element_type=jnp.float32) + bias[...]
    )
    value_part, slope_part = gelu_parts(before)
    hidden = value_part.astype(jnp.bfloat16)
    hidden_out[...] = hidden
    mixed[...] += jnp.dot(hidden, proj[...], preferred_element_type=jnp.float32)
    across = (((1,), (1,)), ((), ()))
    hidden_grad = lax.dot_general(
        cot[...], proj[...], across, preferred_element_type=jnp.float32
    )
    pre_grad = (hidden_grad * slope_part).astype(jnp.bfloat16)
    pre_out[...] = pre_grad
    bias_out[...] = jnp.sum(pre_grad.astype(jnp.float32), axis=0, keepdims=True)
    second_grad[...] += lax.dot_general(
        pre_grad, wide[...], across, preferred_element_type=jnp.float32
    )


def mlp_both(second_in, cot, wide_full, proj_full, fc_bias):
    rows = second_in.shape[0]
    skip = 4 * D // MLP_TILE
    whole = pl.BlockSpec((rows, D), lambda k: (0, 0))
    tile = pl.BlockSpec((rows, MLP_TILE), lambda k: (0, k))
    line = pl.BlockSpec((1, MLP_TILE), lambda k: (0, k))
    return pl.pallas_call(
        mlp_kernel,
        grid=(FF // MLP_TILE,),
        in_specs=[
            whole,
            whole,
            pl.BlockSpec((D, MLP_TILE), lambda k: (0, k + skip)),
            pl.BlockSpec((MLP_TILE, D), lambda k: (k, 0)),
            line,
        ],
        out_specs=(tile, tile, whole, whole, line),
        out_shape=(
            jax.ShapeDtypeStruct((rows, FF), jnp.bfloat16),
            jax.ShapeDtypeStruct((rows, FF), jnp.bfloat16),
            jax.ShapeDtypeStruct((rows, D), jnp.float32),
            jax.ShapeDtypeStruct((rows, D), jnp.float32),
            jax.ShapeDtypeStruct((1, FF), jnp.float32),
        ),
        compiler_params=pltpu.CompilerParams(vmem_limit_bytes=32 * 2**20),
    )(second_in, cot, wide_full, proj_full, fc_bias.reshape(1, FF))


def body(
    tokens,
    seq_lengths,
    cotangent,
    wide_weights,
    proj_weights,
    vector_params,
    wide_moments,
    proj_moments,
    vector_moments,
):
    shards = (
        wide_weights.astype(jnp.bfloat16),
        proj_weights.astype(jnp.bfloat16),
        vector_params.astype(jnp.bfloat16),
    )
    devices = lax.axis_size("fsdp")
    direct = wide_weights.shape[0] == GROUP and devices % 8 == 0
    vector_rows, vector_columns = vector_params.shape
    if direct:
        wide_full, proj_full, vector_tiles = gather_all(
            devices, shards[0], shards[1], to_tile(shards[2].astype(jnp.float32)[None])[0]
        )
        vector_full = (
            from_tile(vector_tiles, vector_rows, vector_columns)
            .transpose(1, 0, 2)
            .reshape(vector_rows, devices * vector_columns)
        )
    else:
        wide_full, proj_full, vector_full = (
            lax.all_gather(shards[0], "fsdp", axis=0, tiled=True),
            lax.all_gather(shards[1], "fsdp", axis=0, tiled=True),
            lax.all_gather(shards[2], "fsdp", axis=1, tiled=True),
        )
    vectors = vector_full.astype(jnp.float32)
    row_count = tokens.shape[0]
    allowed = allowed_pairs(seq_lengths[0], row_count)
    ratio = FF // D
    local_rows = wide_weights.shape[0]
    unscale = math.sqrt(lax.axis_size("fsdp") * row_count)
    gain_one, shift_one, query_bias, value_bias = (vectors[0], vectors[1], vectors[2], vectors[3])
    out_bias, gain_two, shift_two, proj_bias = (vectors[4], vectors[5], vectors[6], vectors[7])
    fc_bias = vectors[8:].reshape(FF)
    token_float = tokens.astype(jnp.float32)
    first_norm, normed_one, inverse_one = norm_forward(token_float, gain_one, shift_one)
    first_in = first_norm.astype(jnp.bfloat16)
    qkv_bias = jnp.concatenate([query_bias, jnp.zeros_like(query_bias), value_bias])
    qkv_half = (
        jnp.dot(first_in, wide_full[:, : 3 * D], preferred_element_type=jnp.float32) + qkv_bias
    ).astype(jnp.bfloat16)
    queries = qkv_half[:, :D]
    key_rows = qkv_half[:, D : 2 * D]
    value_rows = qkv_half[:, 2 * D :]
    attended, logsum = attention_forward(queries, key_rows, value_rows, allowed)
    residual = (
        token_float
        + jnp.dot(attended, wide_full[:, 3 * D : 4 * D], preferred_element_type=jnp.float32)
        + out_bias
    )
    second_norm, normed_two, inverse_two = norm_forward(residual, gain_two, shift_two)
    second_in = second_norm.astype(jnp.bfloat16)
    hidden, pre_grad, mixed, second_grad, fc_bias_sum = mlp_both(
        second_in, cotangent, wide_full, proj_full, fc_bias
    )
    block_output = (residual + mixed + proj_bias).astype(jnp.bfloat16)
    backward_wide, backward_proj, vector_again = wide_full, proj_full, vector_full
    backward_vectors = vector_again.astype(jnp.float32)
    qkv_back = backward_wide[:, : 3 * D]
    out_back = backward_wide[:, 3 * D : 4 * D]
    cot_float = cotangent.astype(jnp.float32)
    proj_bias_grad = jnp.sum(cot_float, axis=0)
    resid_norm_grad, gain_two_grad, shift_two_grad = norm_backward(
        second_grad, normed_two, inverse_two, backward_vectors[5]
    )
    resid_grad = cot_float + resid_norm_grad
    mlp_vectors = jnp.concatenate(
        [
            jnp.stack([gain_two_grad, shift_two_grad, proj_bias_grad]),
            fc_bias_sum.reshape(ratio, D),
        ],
        axis=0,
    )
    resid_half = resid_grad.astype(jnp.bfloat16)
    out_bias_grad = jnp.sum(resid_grad, axis=0)
    attended_grad = jnp.einsum(
        "te,de->td", resid_half, out_back, preferred_element_type=jnp.float32
    ).astype(jnp.bfloat16)
    qkv_grad = attention_backward(queries, key_rows, value_rows, allowed, logsum, attended_grad)
    query_bias_grad = jnp.sum(qkv_grad[:, :D], axis=0, dtype=jnp.float32)
    value_bias_grad = jnp.sum(qkv_grad[:, 2 * D :], axis=0, dtype=jnp.float32)
    first_grad = jnp.einsum("tc,dc->td", qkv_grad, qkv_back, preferred_element_type=jnp.float32)
    token_norm_grad, gain_one_grad, shift_one_grad = norm_backward(
        first_grad, normed_one, inverse_one, backward_vectors[0]
    )
    tokens_grad = (resid_grad + token_norm_grad).astype(jnp.bfloat16)
    attn_vectors = jnp.stack(
        [gain_one_grad, shift_one_grad, query_bias_grad, value_bias_grad, out_bias_grad]
    )
    vector_terms = jnp.concatenate([attn_vectors, mlp_vectors], axis=0)
    if direct:
        owned = vector_terms.reshape(vector_rows, devices, vector_columns).transpose(1, 0, 2)
        wide_grad, proj_grad, vector_tile = scatter_all(
            devices,
            first_in,
            attended,
            second_in,
            hidden,
            qkv_grad,
            resid_half,
            pre_grad,
            cotangent,
            to_tile(owned),
        )
        vector_grad = from_tile(vector_tile[None], vector_rows, vector_columns)[0]
    else:
        fc_part = column_term(second_in, pre_grad)
        proj_part = column_term(hidden, cotangent).reshape(
            local_rows * lax.axis_size("fsdp"), ratio * D
        )
        qkv_part = column_term(first_in, qkv_grad)
        out_part = column_term(attended, resid_half)
        joined_shard = lax.psum_scatter(
            jnp.concatenate(
                [
                    jnp.concatenate([qkv_part, out_part], axis=1),
                    jnp.concatenate([fc_part, proj_part], axis=1),
                ],
                axis=1,
            ),
            "fsdp",
            scatter_dimension=0,
            tiled=True,
        )
        wide_grad = joined_shard[:, : 4 * D + FF]
        proj_grad = joined_shard[:, 4 * D + FF :].reshape(local_rows * ratio, D)
        vector_grad = lax.psum_scatter(vector_terms, "fsdp", scatter_dimension=1, tiled=True)
    wide_new, wide_moments_new = adam_update(
        wide_weights, wide_moments, wide_grad, rate_matrix, weight_decay, unscale
    )
    proj_new, proj_moments_new = adam_update(
        proj_weights, proj_moments, proj_grad, rate_matrix, weight_decay, unscale
    )
    vector_new, vector_moments_new = adam_update(
        vector_params, vector_moments, vector_grad, rate_vector, 0.0, unscale
    )
    return (
        block_output,
        tokens_grad,
        wide_grad,
        proj_grad,
        vector_grad,
        wide_new,
        proj_new,
        vector_new,
        wide_moments_new,
        proj_moments_new,
        vector_moments_new,
    )


def solution(mesh):
    placed = (
        P("fsdp", None),
        P("fsdp", None),
        P("fsdp", None),
        P("fsdp", None),
        P("fsdp", None),
        P(None, "fsdp"),
        P(None, "fsdp", None),
        P(None, "fsdp", None),
        P(None, None, "fsdp"),
    )
    return jax.shard_map(
        body,
        mesh=mesh,
        in_specs=placed,
        out_specs=(
            P("fsdp", None),
            P("fsdp", None),
            P("fsdp", None),
            P("fsdp", None),
            P(None, "fsdp"),
            P("fsdp", None),
            P("fsdp", None),
            P(None, "fsdp"),
            P(None, "fsdp", None),
            P(None, "fsdp", None),
            P(None, None, "fsdp"),
        ),
        check_vma=False,
    )
```
